128 devices in a mesh: comp: 2 (over core), tile: 64 (over x, z, y).
Axes of the slice: x: 4, y: 4, z: 4, core: 2. Of those that a mesh axis runs over, the one named last changes fastest.
Arguments:
- state: float32 [2, 1024, 256], P('comp', 'tile'), may hold values from -6 to 6
- coeff: float32 [2, 1024, 256], P('comp', 'tile'), may hold values from 0.3 to 3
- vertical: int32 [1024, 256], P('tile'), may hold values from 0 to 5
- send_cell: int32 [1024, 4096], P(('comp', 'tile')), may hold values from 0 to 4095, as said below
- incoming_marine_slot: int32 [1024, 4096], P(('comp', 'tile')), may hold values from 0 to 4095, as said below
- remap_weight: float32 [1024, 4096], P(('comp', 'tile')), as said below
Outputs:
- exchanged_pair: float32 [2, 1024, 256], P('comp', 'tile')
The draws below stay inside these ranges and needn't reach their ends.
Inputs may be any that keep to these rules, and one draw needn't show every extreme that they name: `send_cell`: rows of ocean partitions (index 512 and above) are 0. Rows d = 3 and d = 5 of every atmosphere partition are full; rows 0 and 1, 2 and 4, 6 and 7 come in pairs whose live slots fill one row together. Live slots lead each row; dead slots hold cell 0. Every atmosphere cell is named by exactly five live slots of its partition. `incoming_marine_slot`: rows of atmosphere partitions are 0. Row (64 + t) * 8 + d names the ocean cell of the slot that send_cell row ((t - d + 4) mod 64) * 8 + d names; dead slots hold 0. `remap_weight`: live slots have weights of at least 0.25; dead slots and rows of ocean partitions 0.
All inputs are finite; a program needn't handle non-finite values.
Results may differ from the reference program's by a relative error of at most 0.00002.
Values sent between devices are 32-bit elements; how exact they have to be, the bound alone decides.
A program may use at most 64 MiB of HBM per device.

```python
import math
import jax
import jax.numpy as jnp

SIDE_LENGTH = 256
SPAN = 8
SWEEPS = 20
DOMAIN_PIECES = 64
PEERS = 128
MESH_LINES = 1024
BLOCK_POINTS = 4096


def intersection_tables(key):
    base = jax.random.fold_in(key, 4111)
    k_cut, k_cell, k_shift, k_weight, k_perm = jax.random.split(base, 5)
    cuts = jax.random.randint(k_cut, (DOMAIN_PIECES, 3), 0, BLOCK_POINTS // 2 + 1)
    full = jnp.full((DOMAIN_PIECES, 1), BLOCK_POINTS, jnp.int32)
    counts = jnp.concatenate([BLOCK_POINTS - cuts[:, 0:1], cuts[:, 0:1], BLOCK_POINTS - cuts[:, 1:2], full, cuts[:, 1:2], full, BLOCK_POINTS - cuts[:, 2:3], cuts[:, 2:3]], axis=1)
    starts = jnp.cumsum(counts, axis=1) - counts
    slot = jnp.arange(BLOCK_POINTS, dtype=jnp.int32)
    live = slot[None, None, :] < counts[:, :, None]
    order_ids = jnp.clip((starts[:, :, None] + slot[None, None, :]) // 5, 0, BLOCK_POINTS - 1).astype(jnp.int32)
    perm_keys = jax.random.split(k_perm, DOMAIN_PIECES)
    shuffles = jax.vmap(lambda one_key: jax.random.permutation(one_key, BLOCK_POINTS))(perm_keys).astype(jnp.int32)
    permuted = jnp.take_along_axis(shuffles, order_ids.reshape(DOMAIN_PIECES, SPAN * BLOCK_POINTS), axis=1).reshape(DOMAIN_PIECES, SPAN, BLOCK_POINTS)
    atm_cell = jnp.where(live, permuted, 0)
    shift = jax.random.randint(k_shift, (DOMAIN_PIECES, 1), 0, BLOCK_POINTS)
    random_cells = jax.random.randint(k_cell, (DOMAIN_PIECES, SPAN, BLOCK_POINTS), 0, BLOCK_POINTS)
    first_cells = (slot[None, :] + shift) % BLOCK_POINTS
    ocean_cell = jnp.where(live, random_cells.at[:, 0, :].set(first_cells), 0)
    weight = jnp.where(live, jax.random.uniform(k_weight, (DOMAIN_PIECES, SPAN, BLOCK_POINTS), jnp.float32, 0.25, 1.0), 0.0)
    tile_ids = jnp.arange(DOMAIN_PIECES, dtype=jnp.int32)[:, None]
    offset_ids = jnp.arange(SPAN, dtype=jnp.int32)[None, :]
    source = (tile_ids - offset_ids + SPAN // 2) % DOMAIN_PIECES
    ocean_rows = ocean_cell[source, offset_ids]
    zero_int = jnp.zeros((DOMAIN_PIECES, SPAN, BLOCK_POINTS), jnp.int32)
    sends = jnp.concatenate([atm_cell, zero_int], axis=0)
    arrived_numbers = jnp.concatenate([zero_int, ocean_rows], axis=0)
    weights = jnp.concatenate([weight, jnp.zeros((DOMAIN_PIECES, SPAN, BLOCK_POINTS), jnp.float32)], axis=0)
    return (sends.reshape(PEERS * SPAN, BLOCK_POINTS), arrived_numbers.reshape(PEERS * SPAN, BLOCK_POINTS), weights.reshape(PEERS * SPAN, BLOCK_POINTS))


def draw_send_cell(key, part):
    return intersection_tables(key)[0]


def draw_incoming_marine_slot(key, part):
    return intersection_tables(key)[1]


def draw_remap_weight(key, part):
    return intersection_tables(key)[2]


def touch_ends(result, stream_key, least, top_value):
    longest = result.shape.index(max(result.shape))
    spots = []
    for shift in (0, 1):
        where = [jax.random.randint(jax.random.fold_in(stream_key, axis), (), 0, length) for axis, length in enumerate(result.shape)]
        where[longest] = (where[longest] + shift) % result.shape[longest]
        spots.append(tuple(where))
    return result.at[spots[0]].set(least).at[spots[1]].set(top_value)


def steps_of(own_key, shape, shards, least, largest):
    def one(axis_at, shards_of):
        steps = jax.random.uniform(jax.random.fold_in(jax.random.fold_in(own_key, 6), axis_at), (shards_of,), jnp.float32, least / len(shards), largest / len(shards))
        return jnp.repeat(jnp.exp(steps), shape[axis_at] // shards_of).reshape((-1,) + (1,) * (len(shape) - axis_at - 1))

    gain = one(*shards[0])
    for cut in shards[1:]:
        gain = gain * one(*cut)
    return gain


def centred(key, shape, width, limit, cuts=(), kind=jnp.bfloat16):
    loudness = steps_of(key, shape, cuts, -0.22, 0.18) if cuts else 1.0
    values = jax.random.normal(key, shape, jnp.float32) * width * loudness
    return jnp.minimum(jnp.maximum(values, -limit), limit).astype(kind)


def setup_inputs(seed: int = 0) -> dict:
    keys = jax.random.split(jax.random.key(seed), 7)
    state = centred(keys[0], (2, MESH_LINES, SIDE_LENGTH), 1.0, 6.0, ((0, 2), (1, 64)), jnp.float32)
    coeff = jnp.clip(jnp.exp(math.log(3.0) - 2.3025851 * jax.random.uniform(keys[1], (2, MESH_LINES, SIDE_LENGTH), jnp.float32) ** steps_of(keys[1], (2, MESH_LINES, SIDE_LENGTH), ((0, 2), (1, 64)), -0.2, 0.2)), 0.3, 3.0)
    vertical = touch_ends(jax.random.randint(keys[2], (MESH_LINES, SIDE_LENGTH), 0, 6), jax.random.fold_in(keys[2], 1), 0, 5).astype(jnp.int32)
    send_cell = draw_send_cell(jax.random.fold_in(keys[6], 71), 0)
    incoming_marine_slot = draw_incoming_marine_slot(jax.random.fold_in(keys[6], 71), 0)
    remap_weight = draw_remap_weight(jax.random.fold_in(keys[6], 71), 0)
    return dict(state=state, coeff=coeff, vertical=vertical, send_cell=send_cell, incoming_marine_slot=incoming_marine_slot, remap_weight=remap_weight)


def reference(state, coeff, vertical, send_cell, incoming_marine_slot, remap_weight):
    air = state[0]
    marine_solution = state[1]
    near = jnp.roll(air, 1, 0) + jnp.roll(air, -1, 0) + jnp.roll(air, 1, 1) + jnp.roll(air, -1, 1)
    air_flux = (coeff[0] * (air + 0.2 * (near - 4.0 * air))).reshape(DOMAIN_PIECES, BLOCK_POINTS)
    sends = send_cell.reshape(PEERS, SPAN, BLOCK_POINTS)[:DOMAIN_PIECES]
    weights = remap_weight.reshape(PEERS, SPAN, BLOCK_POINTS)[:DOMAIN_PIECES]
    ocean_rows = incoming_marine_slot.reshape(PEERS, SPAN, BLOCK_POINTS)[DOMAIN_PIECES:]
    source_ids = jnp.arange(DOMAIN_PIECES, dtype=jnp.int32)
    offset_ids = jnp.arange(SPAN, dtype=jnp.int32)
    target_model = ((source_ids[:, None] + offset_ids[None, :] - SPAN // 2) % DOMAIN_PIECES).astype(jnp.int32)
    arrived_numbers = ocean_rows[target_model, offset_ids[None, :]]
    picked = air_flux[source_ids[:, None, None], sends]
    ocean_flat = (target_model[:, :, None] * BLOCK_POINTS + arrived_numbers).astype(jnp.int32)
    ocean_source = jnp.zeros((DOMAIN_PIECES * BLOCK_POINTS,), jnp.float32).at[ocean_flat.reshape(-1)].add((weights * picked).reshape(-1))
    source_mesh = ocean_source.reshape(MESH_LINES, SIDE_LENGTH)
    rhs = source_mesh + marine_solution
    diag = coeff[1] + 3.0
    row_ids = jnp.arange(MESH_LINES, dtype=jnp.int32)[:, None]
    col_ids = jnp.arange(SIDE_LENGTH, dtype=jnp.int32)[None, :]
    up_down = vertical // 3
    sideways = vertical % 3 - 1
    index = (((row_ids - 1 + 2 * up_down) % MESH_LINES) * SIDE_LENGTH + (col_ids + sideways) % SIDE_LENGTH).astype(jnp.int32)
    elevation_trace = jnp.zeros((MESH_LINES, SIDE_LENGTH), jnp.float32)
    for sweep in range(SWEEPS):
        beside_all = jnp.roll(elevation_trace, 1, 1) + jnp.roll(elevation_trace, -1, 1) + jnp.take(elevation_trace.reshape(-1), index)
        elevation_trace = (rhs + beside_all) / diag
    fresh_skin_heat = (marine_solution + 0.5 * elevation_trace - 0.25 * source_mesh).reshape(DOMAIN_PIECES, BLOCK_POINTS)
    number_listing = fresh_skin_heat[target_model[:, :, None], arrived_numbers]
    air_flat = (source_ids[:, None, None] * BLOCK_POINTS + sends).astype(jnp.int32).reshape(-1)
    share_accumulated = jnp.zeros((DOMAIN_PIECES * BLOCK_POINTS,), jnp.float32).at[air_flat].add(weights.reshape(-1))
    overall_quantity = jnp.zeros((DOMAIN_PIECES * BLOCK_POINTS,), jnp.float32).at[air_flat].add((weights * number_listing).reshape(-1))
    measured_skin_heat = (overall_quantity / share_accumulated).reshape(MESH_LINES, SIDE_LENGTH)
    return jnp.stack([measured_skin_heat, elevation_trace])
```

```python
import functools

import jax
import jax.numpy as jnp
from jax import lax
from jax.experimental import pallas as pl
from jax.experimental.pallas import tpu as pltpu
from jax.sharding import PartitionSpec as P

SPAN = 8
SWEEPS = 20
TILES = 64
ROWS = 16
COLS = 256
CELLS = ROWS * COLS
LANES = 128
BLOCKS = CELLS // LANES
MERGED = ((0, 1), (2, 4), (3, None), (5, None), (6, 7))
OWN = 24
WINDOW = 64
MESH = pl.DeviceIdType.MESH
F32 = jnp.float32
BF16 = jnp.bfloat16


def reverse_tile(x):
    row = 7 - lax.broadcasted_iota(jnp.int32, (8, LANES), 0)
    lane = LANES - 1 - lax.broadcasted_iota(jnp.int32, (8, LANES), 1)
    return jnp.take_along_axis(jnp.take_along_axis(x, row, axis=0), lane, axis=1)


def lookup(table, index):
    lane = index & (LANES - 1)
    bits = [((index >> (7 + b)) & 1) == 1 for b in range(5)]

    def pick(level, base):
        if level < 0:
            row = table[base // 2 : base // 2 + 1, (base % 2) * LANES : (base % 2 + 1) * LANES]
            return jnp.take_along_axis(jnp.broadcast_to(row, (8, LANES)), lane, axis=1)
        low = pick(level - 1, base)
        high = pick(level - 1, base + (1 << level))
        return jnp.where(bits[level], high, low)

    return pick(4, 0)


def spread(row, count):
    piece = jnp.broadcast_to(row.astype(F32), (16, LANES)).astype(BF16)
    return jnp.concatenate([piece] * (count // 16), 0)


def numbers(count):
    return lax.broadcasted_iota(jnp.int32, (count, LANES), 0).astype(F32).astype(BF16)


def scatter_sum(index, value):
    zero, one = jnp.zeros((), BF16), jnp.ones((), BF16)
    lefts, rights = [], []
    for j in range(BLOCKS):
        i, v = index(j), value(j)
        line = ((i >> 7) & 1) * 16 + (i >> 8)
        head = v.astype(BF16).astype(F32)
        here = spread(line, 32) == numbers(32)
        lefts.append(
            jnp.concatenate(
                [
                    jnp.where(here, spread(head, 32), zero),
                    jnp.where(here, spread(v - head, 32), zero),
                ],
                0,
            )
        )
        rights.append(jnp.where(spread(i & (LANES - 1), LANES) == numbers(LANES), one, zero))
    left = jnp.concatenate(lefts, 1)
    right = jnp.concatenate(rights, 1)
    return lax.dot_general(left, right, (((1,), (1,)), ((), ())), preferred_element_type=F32)


def halves(total):
    both = total[0:32] + total[32:64]
    return jnp.concatenate([both[0:16], both[16:32]], axis=1)


def kernel(
    state,
    coeff,
    vertical,
    send_cell,
    marine_slot,
    weight,
    out,
    own,
    rate,
    table,
    codes,
    weights,
    air_halo,
    merged,
    values,
    rows_out,
    rows_in,
    total,
    weight_sum,
    win_rhs,
    win_diag,
    win_code,
    load_sem,
    halo_send,
    halo_recv,
    row_send,
    row_recv,
    rhs_send,
    rhs_recv,
    win_send,
    win_recv,
):
    model = lax.axis_index("comp")
    tile = lax.axis_index("tile")

    def at(offset):
        return lax.rem(tile + offset + TILES, TILES)

    def copy_to(source, target, send, recv, comp, piece):
        return pltpu.make_async_remote_copy(
            src_ref=source,
            dst_ref=target,
            send_sem=send,
            recv_sem=recv,
            device_id=(comp, piece),
            device_id_type=MESH,
        )

    def load(source, target, k):
        return pltpu.make_async_copy(source, target, load_sem.at[k])

    def greet(partners):
        barrier = pltpu.get_barrier_semaphore()
        for comp, piece in partners:
            pl.semaphore_signal(barrier, inc=1, device_id=(comp, piece), device_id_type=MESH)
        pl.semaphore_wait(barrier, len(partners))

    def to_ocean(d):
        return copy_to(rows_out.at[d], rows_in.at[d], row_send.at[d], row_recv.at[d], 1, at(d - 4))

    def to_air(d):
        return copy_to(rows_out.at[d], rows_in.at[d], row_send.at[d], row_recv.at[d], 0, at(4 - d))

    def slab(ref, d, q):
        return ref[pl.ds(64 * q + d, 8, stride=8), :]

    @pl.when(model == 0)
    def _():
        loads = [
            load(send_cell, codes, 0),
            load(weight, weights, 1),
            load(state.at[0], own, 2),
            load(coeff.at[0], rate, 3),
        ]
        for item in loads:
            item.start()
        greet([(0, at(1)), (0, at(-1))] + [(1, at(d - 4)) for d in range(SPAN)])
        down = copy_to(
            state.at[0, pl.ds(8, 8)], air_halo.at[0], halo_send.at[0], halo_recv.at[0], 0, at(1)
        )
        up = copy_to(
            state.at[0, pl.ds(0, 8)], air_halo.at[1], halo_send.at[1], halo_recv.at[1], 0, at(-1)
        )
        down.start()
        up.start()
        for item in loads:
            item.wait()
        for m, (d, e) in enumerate(MERGED):
            for q in range(4):
                index = slab(codes, d, q)
                if e is not None:
                    index = index + reverse_tile(slab(codes, e, 3 - q))
                merged[m, 8 * q : 8 * q + 8, :] = index
        down.wait_recv()
        up.wait_recv()
        s = own[...]
        row_id = lax.broadcasted_iota(jnp.int32, (ROWS, COLS), 0)
        above = jnp.where(row_id == 0, air_halo[0, 7:8, :], pltpu.roll(s, 1, 0))
        below = jnp.where(row_id == ROWS - 1, air_halo[1, 0:1, :], pltpu.roll(s, ROWS - 1, 0))
        near = above + below + pltpu.roll(s, 1, 1) + pltpu.roll(s, COLS - 1, 1)
        table[...] = rate[...] * (s + 0.2 * (near - 4.0 * s))
        for m, (d, e) in enumerate(MERGED):
            for q in range(4):
                found = lookup(table, merged[m, 8 * q : 8 * q + 8, :])
                rows_out[d, 8 * q : 8 * q + 8, :] = slab(weights, d, q) * found
                if e is not None:
                    p = 3 - q
                    rows_out[e, 8 * p : 8 * p + 8, :] = slab(weights, e, p) * reverse_tile(found)
            to_ocean(d).start()
            if e is not None:
                to_ocean(e).start()
        for m, (d, e) in enumerate(MERGED):
            for q in range(4):
                w = slab(weights, d, q)
                if e is not None:
                    w = w + reverse_tile(slab(weights, e, 3 - q))
                values[m, 8 * q : 8 * q + 8, :] = w
        weight_sum[...] = jnp.zeros_like(weight_sum)
        total[...] = jnp.zeros_like(total)

        @pl.loop(0, len(MERGED))
        def _(m):
            weight_sum[...] += scatter_sum(
                lambda j: merged[m, j : j + 1, :], lambda j: values[m, j : j + 1, :]
            )

        for m, (d, e) in enumerate(MERGED):
            to_air(d).wait_recv()
            if e is not None:
                to_air(e).wait_recv()
            for q in range(4):
                v = slab(weights, d, q) * rows_in[d, 8 * q : 8 * q + 8, :]
                if e is not None:
                    p = 3 - q
                    v = v + reverse_tile(slab(weights, e, p) * rows_in[e, 8 * p : 8 * p + 8, :])
                values[m, 8 * q : 8 * q + 8, :] = v
            total[...] += scatter_sum(
                lambda j: merged[m, j : j + 1, :], lambda j: values[m, j : j + 1, :]
            )
        out[...] = halves(total[...]) / halves(weight_sum[...])
        down.wait_send()
        up.wait_send()
        for d in range(SPAN):
            to_ocean(d).wait_send()

    @pl.when(model == 1)
    def _():
        mine = pl.ds(OWN, ROWS)
        loads = [
            load(marine_slot, codes, 0),
            load(state.at[0], own, 1),
            load(coeff.at[0], win_diag.at[mine], 2),
            load(vertical, win_code.at[mine], 3),
        ]
        for item in loads:
            item.start()
        greet(
            [(1, at(1)), (1, at(-1)), (1, at(2)), (1, at(-2))]
            + [(0, at(4 - d)) for d in range(SPAN)]
        )

        def to_windows(source, target, send, recv):
            return [
                copy_to(
                    source(first, rows),
                    target.at[pl.ds(place, rows)],
                    send.at[k],
                    recv.at[k],
                    1,
                    at(offset),
                )
                for k, (offset, first, rows, place) in enumerate(
                    (
                        (1, 0, 16, OWN - 16),
                        (-1, 0, 16, OWN + 16),
                        (2, 8, 8, OWN - 24),
                        (-2, 0, 8, OWN + 32),
                    )
                )
            ]

        ahead = to_windows(
            lambda first, rows: coeff.at[0, pl.ds(first, rows)],
            win_diag,
            win_send.at[0],
            win_recv.at[0],
        ) + to_windows(
            lambda first, rows: vertical.at[pl.ds(first, rows)],
            win_code,
            win_send.at[1],
            win_recv.at[1],
        )
        for item in ahead:
            item.start()
        for item in loads:
            item.wait()
        for item in ahead:
            item.wait_recv()
        total[...] = jnp.zeros_like(total)

        @pl.loop(0, SPAN)
        def _(d):
            to_ocean(d).wait_recv()
            total[...] += scatter_sum(
                lambda j: codes[pl.ds(8 * j + d, 1), :], lambda j: rows_in[d, j : j + 1, :]
            )

        source = halves(total[...])
        win_rhs[mine, :] = source + own[...]
        sides = to_windows(
            lambda first, rows: win_rhs.at[pl.ds(OWN + first, rows)], win_rhs, rhs_send, rhs_recv
        )
        for item in sides:
            item.start()
        for item in sides:
            item.wait_recv()

        def sweeps(eta, count, margin):
            rows = WINDOW - 2 * margin
            part = pl.ds(margin, rows)
            first = eta[margin_of(eta, rows) : margin_of(eta, rows) + rows]
            code = win_code[part, :]
            far = code >= 3
            side = code - jnp.where(far, 3, 0)
            from_up = pltpu.roll(side, rows - 1, 0)
            from_down = pltpu.roll(side, 1, 0)
            scale = 1.0 / (win_diag[part, :] + 3.0)
            rhs = win_rhs[part, :]

            def one(_, x):
                left = pltpu.roll(x, 1, 1)
                right = pltpu.roll(x, COLS - 1, 1)
                up = jnp.where(from_up == 0, left, jnp.where(from_up == 1, x, right))
                down = jnp.where(from_down == 0, left, jnp.where(from_down == 1, x, right))
                third = jnp.where(far, pltpu.roll(down, rows - 1, 0), pltpu.roll(up, 1, 0))
                return (rhs + (left + right + third)) * scale

            return lax.fori_loop(0, count, one, first)

        def margin_of(x, rows):
            return (x.shape[0] - rows) // 2

        eta = win_rhs[...] / (win_diag[...] + 3.0)
        eta = sweeps(eta, 3, 0)
        eta = sweeps(eta, 8, 8)
        eta = sweeps(eta, 8, 16)
        eta = eta[8:24]
        out[...] = eta
        table[...] = own[...] + 0.5 * eta - 0.25 * source
        for d in range(SPAN):
            for q in range(4):
                rows_out[d, 8 * q : 8 * q + 8, :] = lookup(table, slab(codes, d, q))
            to_air(d).start()
        for item in ahead + sides:
            item.wait_send()
        for d in range(SPAN):
            to_air(d).wait_send()


def shards(state, coeff, vertical, send_cell, incoming_marine_slot, remap_weight):
    def blocks(x):
        return x.reshape(SPAN, BLOCKS, LANES).transpose(1, 0, 2).reshape(SPAN * BLOCKS, LANES)

    anywhere = pl.BlockSpec(memory_space=pl.ANY)
    grid = pltpu.VMEM((ROWS, COLS), F32)
    dma = pltpu.SemaphoreType.DMA
    result = pl.pallas_call(
        kernel,
        out_shape=jax.ShapeDtypeStruct((ROWS, COLS), F32),
        in_specs=[anywhere] * 6,
        out_specs=pl.BlockSpec(memory_space=pltpu.VMEM),
        scratch_shapes=[
            grid,
            grid,
            grid,
            pltpu.VMEM((SPAN * BLOCKS, LANES), jnp.int32),
            pltpu.VMEM((SPAN * BLOCKS, LANES), F32),
            pltpu.VMEM((2, 8, COLS), F32),
            pltpu.VMEM((len(MERGED), BLOCKS, LANES), jnp.int32),
            pltpu.VMEM((len(MERGED), BLOCKS, LANES), F32),
            pltpu.VMEM((SPAN, BLOCKS, LANES), F32),
            pltpu.VMEM((SPAN, BLOCKS, LANES), F32),
            pltpu.VMEM((64, LANES), F32),
            pltpu.VMEM((64, LANES), F32),
            pltpu.VMEM((WINDOW, COLS), F32),
            pltpu.VMEM((WINDOW, COLS), F32),
            pltpu.VMEM((WINDOW, COLS), jnp.int32),
            dma((4,)),
            dma((2,)),
            dma((2,)),
            dma((SPAN,)),
            dma((SPAN,)),
            dma((4,)),
            dma((4,)),
            dma((2, 4)),
            dma((2, 4)),
        ],
        compiler_params=pltpu.CompilerParams(
            collective_id=0, has_side_effects=True, vmem_limit_bytes=40 << 20
        ),
    )(
        state,
        coeff,
        vertical,
        blocks(send_cell),
        blocks(incoming_marine_slot),
        blocks(remap_weight),
    )
    return result[None]


def solution(mesh):
    in_specs = (
        P("comp", "tile", None),
        P("comp", "tile", None),
        P("tile", None),
        P(("comp", "tile"), None),
        P(("comp", "tile"), None),
        P(("comp", "tile"), None),
    )
    out_specs = P("comp", "tile", None)
    return jax.shard_map(shards, mesh=mesh, in_specs=in_specs, out_specs=out_specs, check_vma=False)
```

```python
import functools

import jax
import jax.numpy as jnp
from jax import lax
from jax.experimental import pallas as pl
from jax.experimental.pallas import tpu as pltpu
from jax.sharding import PartitionSpec as P

SPAN = 8
SWEEPS = 20
TILES = 64
ROWS = 16
COLS = 256
CELLS = ROWS * COLS
LANES = 128
BLOCKS = CELLS // LANES
MERGED = ((0, 1), (2, 4), (3, None), (5, None), (6, 7))
OWN = 24
WINDOW = 64
MESH = pl.DeviceIdType.MESH
F32 = jnp.float32
BF16 = jnp.bfloat16


def reverse_tile(x):
    row = 7 - lax.broadcasted_iota(jnp.int32, (8, LANES), 0)
    lane = LANES - 1 - lax.broadcasted_iota(jnp.int32, (8, LANES), 1)
    return jnp.take_along_axis(jnp.take_along_axis(x, row, axis=0), lane, axis=1)


def lookup(table, index):
    lane = index & (LANES - 1)
    bits = [((index >> (7 + b)) & 1) == 1 for b in range(5)]

    def pick(level, base):
        if level < 0:
            row = table[base // 2 : base // 2 + 1, (base % 2) * LANES : (base % 2 + 1) * LANES]
            return jnp.take_along_axis(jnp.broadcast_to(row, (8, LANES)), lane, axis=1)
        low = pick(level - 1, base)
        high = pick(level - 1, base + (1 << level))
        return jnp.where(bits[level], high, low)

    return pick(4, 0)


def spread(row, count):
    piece = jnp.broadcast_to(row.astype(F32), (16, LANES)).astype(BF16)
    return jnp.concatenate([piece] * (count // 16), 0)


def numbers(count):
    return lax.broadcasted_iota(jnp.int32, (count, LANES), 0).astype(F32).astype(BF16)


def scatter_sum(index, value):
    zero, one = jnp.zeros((), BF16), jnp.ones((), BF16)
    lefts, rights = [], []
    for j in range(BLOCKS):
        i, v = index(j), value(j)
        line = ((i >> 7) & 1) * 16 + (i >> 8)
        head = v.astype(BF16).astype(F32)
        here = spread(line, 32) == numbers(32)
        lefts.append(
            jnp.concatenate(
                [
                    jnp.where(here, spread(head, 32), zero),
                    jnp.where(here, spread(v - head, 32), zero),
                ],
                0,
            )
        )
        rights.append(jnp.where(spread(i & (LANES - 1), LANES) == numbers(LANES), one, zero))
    left = jnp.concatenate(lefts, 1)
    right = jnp.concatenate(rights, 1)
    return lax.dot_general(left, right, (((1,), (1,)), ((), ())), preferred_element_type=F32)


def halves(total):
    both = total[0:32] + total[32:64]
    return jnp.concatenate([both[0:16], both[16:32]], axis=1)


def kernel(
    state,
    coeff,
    vertical,
    send_cell,
    marine_slot,
    weight,
    out,
    own,
    rate,
    table,
    codes,
    weights,
    air_halo,
    merged,
    values,
    rows_out,
    rows_in,
    total,
    weight_sum,
    win_rhs,
    win_diag,
    win_code,
    load_sem,
    halo_send,
    halo_recv,
    row_send,
    row_recv,
    rhs_send,
    rhs_recv,
    win_send,
    win_recv,
):
    model = lax.axis_index("comp")
    tile = lax.axis_index("tile")

    def at(offset):
        return lax.rem(tile + offset + TILES, TILES)

    def copy_to(source, target, send, recv, comp, piece):
        return pltpu.make_async_remote_copy(
            src_ref=source,
            dst_ref=target,
            send_sem=send,
            recv_sem=recv,
            device_id=(comp, piece),
            device_id_type=MESH,
        )

    def load(source, target, k):
        return pltpu.make_async_copy(source, target, load_sem.at[k])

    def greet(partners):
        barrier = pltpu.get_barrier_semaphore()
        for comp, piece in partners:
            pl.semaphore_signal(barrier, inc=1, device_id=(comp, piece), device_id_type=MESH)
        pl.semaphore_wait(barrier, len(partners))

    def to_ocean(d):
        return copy_to(rows_out.at[d], rows_in.at[d], row_send.at[d], row_recv.at[d], 1, at(d - 4))

    def to_air(d):
        return copy_to(rows_out.at[d], rows_in.at[d], row_send.at[d], row_recv.at[d], 0, at(4 - d))

    def slab(ref, d, q):
        return ref[pl.ds(64 * q + d, 8, stride=8), :]

    @pl.when(model == 0)
    def _():
        loads = [
            load(send_cell, codes, 0),
            load(weight, weights, 1),
            load(state.at[0], own, 2),
            load(coeff.at[0], rate, 3),
        ]
        for item in loads:
            item.start()
        greet([(0, at(1)), (0, at(-1))] + [(1, at(d - 4)) for d in range(SPAN)])
        down = copy_to(
            state.at[0, pl.ds(8, 8)], air_halo.at[0], halo_send.at[0], halo_recv.at[0], 0, at(1)
        )
        up = copy_to(
            state.at[0, pl.ds(0, 8)], air_halo.at[1], halo_send.at[1], halo_recv.at[1], 0, at(-1)
        )
        down.start()
        up.start()
        for item in loads:
            item.wait()
        for m, (d, e) in enumerate(MERGED):
            for q in range(4):
                index = slab(codes, d, q)
                if e is not None:
                    index = index + reverse_tile(slab(codes, e, 3 - q))
                merged[m, 8 * q : 8 * q + 8, :] = index
        down.wait_recv()
        up.wait_recv()
        s = own[...]
        row_id = lax.broadcasted_iota(jnp.int32, (ROWS, COLS), 0)
        above = jnp.where(row_id == 0, air_halo[0, 7:8, :], pltpu.roll(s, 1, 0))
        below = jnp.where(row_id == ROWS - 1, air_halo[1, 0:1, :], pltpu.roll(s, ROWS - 1, 0))
        near = above + below + pltpu.roll(s, 1, 1) + pltpu.roll(s, COLS - 1, 1)
        table[...] = rate[...] * (s + 0.2 * (near - 4.0 * s))
        for m, (d, e) in enumerate(MERGED):
            for q in range(4):
                found = lookup(table, merged[m, 8 * q : 8 * q + 8, :])
                rows_out[d, 8 * q : 8 * q + 8, :] = slab(weights, d, q) * found
                if e is not None:
                    p = 3 - q
                    rows_out[e, 8 * p : 8 * p + 8, :] = slab(weights, e, p) * reverse_tile(found)
            to_ocean(d).start()
            if e is not None:
                to_ocean(e).start()
        for m, (d, e) in enumerate(MERGED):
            for q in range(4):
                w = slab(weights, d, q)
                if e is not None:
                    w = w + reverse_tile(slab(weights, e, 3 - q))
                values[m, 8 * q : 8 * q + 8, :] = w
        weight_sum[...] = jnp.zeros_like(weight_sum)
        total[...] = jnp.zeros_like(total)

        @pl.loop(0, len(MERGED))
        def _(m):
            weight_sum[...] += scatter_sum(
                lambda j: merged[m, j : j + 1, :], lambda j: values[m, j : j + 1, :]
            )

        for m, (d, e) in enumerate(MERGED):
            to_air(d).wait_recv()
            if e is not None:
                to_air(e).wait_recv()
            for q in range(4):
                v = slab(weights, d, q) * rows_in[d, 8 * q : 8 * q + 8, :]
                if e is not None:
                    p = 3 - q
                    v = v + reverse_tile(slab(weights, e, p) * rows_in[e, 8 * p : 8 * p + 8, :])
                values[m, 8 * q : 8 * q + 8, :] = v
            total[...] += scatter_sum(
                lambda j: merged[m, j : j + 1, :], lambda j: values[m, j : j + 1, :]
            )
        out[...] = halves(total[...]) / halves(weight_sum[...])
        down.wait_send()
        up.wait_send()
        for d in range(SPAN):
            to_ocean(d).wait_send()

    @pl.when(model == 1)
    def _():
        mine = pl.ds(OWN, ROWS)
        loads = [
            load(marine_slot, codes, 0),
            load(state.at[0], own, 1),
            load(coeff.at[0], win_diag.at[mine], 2),
            load(vertical, win_code.at[mine], 3),
        ]
        for item in loads:
            item.start()
        greet(
            [(1, at(1)), (1, at(-1)), (1, at(2)), (1, at(-2))]
            + [(0, at(4 - d)) for d in range(SPAN)]
        )

        def to_windows(source, target, send, recv):
            return [
                copy_to(
                    source(first, rows),
                    target.at[pl.ds(place, rows)],
                    send.at[k],
                    recv.at[k],
                    1,
                    at(offset),
                )
                for k, (offset, first, rows, place) in enumerate(
                    (
                        (1, 0, 16, OWN - 16),
                        (-1, 0, 16, OWN + 16),
                        (2, 8, 8, OWN - 24),
                        (-2, 0, 8, OWN + 32),
                    )
                )
            ]

        ahead = to_windows(
            lambda first, rows: coeff.at[0, pl.ds(first, rows)],
            win_diag,
            win_send.at[0],
            win_recv.at[0],
        ) + to_windows(
            lambda first, rows: vertical.at[pl.ds(first, rows)],
            win_code,
            win_send.at[1],
            win_recv.at[1],
        )
        for item in ahead:
            item.start()
        for item in loads:
            item.wait()
        for item in ahead:
            item.wait_recv()
        total[...] = jnp.zeros_like(total)

        @pl.loop(0, SPAN)
        def _(d):
            to_ocean(d).wait_recv()
            total[...] += scatter_sum(
                lambda j: codes[pl.ds(8 * j + d, 1), :], lambda j: rows_in[d, j : j + 1, :]
            )

        source = halves(total[...])
        win_rhs[mine, :] = source + own[...]
        sides = to_windows(
            lambda first, rows: win_rhs.at[pl.ds(OWN + first, rows)], win_rhs, rhs_send, rhs_recv
        )
        for item in sides:
            item.start()
        for item in sides:
            item.wait_recv()

        def sweeps(eta, count, margin):
            rows = WINDOW - 2 * margin
            part = pl.ds(margin, rows)
            first = eta[margin_of(eta, rows) : margin_of(eta, rows) + rows]
            code = win_code[part, :]
            far = code >= 3
            side = code - jnp.where(far, 3, 0)
            from_up = pltpu.roll(side, rows - 1, 0)
            from_down = pltpu.roll(side, 1, 0)
            scale = 1.0 / (win_diag[part, :] + 3.0)
            rhs = win_rhs[part, :]

            def one(_, x):
                left = pltpu.roll(x, 1, 1)
                right = pltpu.roll(x, COLS - 1, 1)
                up = jnp.where(from_up == 0, left, jnp.where(from_up == 1, x, right))
                down = jnp.where(from_down == 0, left, jnp.where(from_down == 1, x, right))
                third = jnp.where(far, pltpu.roll(down, rows - 1, 0), pltpu.roll(up, 1, 0))
                return (rhs + (left + right + third)) * scale

            return lax.fori_loop(0, count, one, first)

        def margin_of(x, rows):
            return (x.shape[0] - rows) // 2

        eta = win_rhs[...] / (win_diag[...] + 3.0)
        eta = sweeps(eta, 3, 0)
        eta = sweeps(eta, 8, 8)
        eta = sweeps(eta, 8, 16)
        eta = eta[8:24]
        out[...] = eta
        table[...] = own[...] + 0.5 * eta - 0.25 * source
        for d in range(SPAN):
            for q in range(4):
                rows_out[d, 8 * q : 8 * q + 8, :] = lookup(table, slab(codes, d, q))
            to_air(d).start()
        for item in ahead + sides:
            item.wait_send()
        for d in range(SPAN):
            to_air(d).wait_send()


def shards(state, coeff, vertical, send_cell, incoming_marine_slot, remap_weight):
    def blocks(x):
        return x.reshape(SPAN, BLOCKS, LANES).transpose(1, 0, 2).reshape(SPAN * BLOCKS, LANES)

    anywhere = pl.BlockSpec(memory_space=pltpu.HBM)
    grid = pltpu.VMEM((ROWS, COLS), F32)
    dma = pltpu.SemaphoreType.DMA
    result = pl.pallas_call(
        kernel,
        out_shape=jax.ShapeDtypeStruct((ROWS, COLS), F32),
        in_specs=[anywhere] * 6,
        out_specs=pl.BlockSpec(memory_space=pltpu.VMEM),
        scratch_shapes=[
            grid,
            grid,
            grid,
            pltpu.VMEM((SPAN * BLOCKS, LANES), jnp.int32),
            pltpu.VMEM((SPAN * BLOCKS, LANES), F32),
            pltpu.VMEM((2, 8, COLS), F32),
            pltpu.VMEM((len(MERGED), BLOCKS, LANES), jnp.int32),
            pltpu.VMEM((len(MERGED), BLOCKS, LANES), F32),
            pltpu.VMEM((SPAN, BLOCKS, LANES), F32),
            pltpu.VMEM((SPAN, BLOCKS, LANES), F32),
            pltpu.VMEM((64, LANES), F32),
            pltpu.VMEM((64, LANES), F32),
            pltpu.VMEM((WINDOW, COLS), F32),
            pltpu.VMEM((WINDOW, COLS), F32),
            pltpu.VMEM((WINDOW, COLS), jnp.int32),
            dma((4,)),
            dma((2,)),
            dma((2,)),
            dma((SPAN,)),
            dma((SPAN,)),
            dma((4,)),
            dma((4,)),
            dma((2, 4)),
            dma((2, 4)),
        ],
        compiler_params=pltpu.CompilerParams(
            collective_id=0, has_side_effects=True, vmem_limit_bytes=40 << 20
        ),
    )(
        *(
            pltpu.with_memory_space_constraint(x, pltpu.HBM)
            for x in (
                state,
                coeff,
                vertical,
                blocks(send_cell),
                blocks(incoming_marine_slot),
                blocks(remap_weight),
            )
        )
    )
    return result[None]


def solution(mesh):
    in_specs = (
        P("comp", "tile", None),
        P("comp", "tile", None),
        P("tile", None),
        P(("comp", "tile"), None),
        P(("comp", "tile"), None),
        P(("comp", "tile"), None),
    )
    out_specs = P("comp", "tile", None)
    return jax.shard_map(shards, mesh=mesh, in_specs=in_specs, out_specs=out_specs, check_vma=False)
```

```python
import functools

import jax
import jax.numpy as jnp
from jax import lax
from jax.experimental import pallas as pl
from jax.experimental.pallas import tpu as pltpu
from jax.sharding import PartitionSpec as P

SPAN = 8
SWEEPS = 20
TILES = 64
ROWS = 16
COLS = 256
CELLS = ROWS * COLS
LANES = 128
BLOCKS = CELLS // LANES
MERGED = ((0, 1), (2, 4), (3, None), (5, None), (6, 7))
OWN = 24
WINDOW = 64
MESH = pl.DeviceIdType.MESH
F32 = jnp.float32
BF16 = jnp.bfloat16


def reverse_tile(x):
    row = 7 - lax.broadcasted_iota(jnp.int32, (8, LANES), 0)
    lane = LANES - 1 - lax.broadcasted_iota(jnp.int32, (8, LANES), 1)
    return jnp.take_along_axis(jnp.take_along_axis(x, row, axis=0), lane, axis=1)


def lookup(table, index):
    lane = index & (LANES - 1)
    bits = [((index >> (7 + b)) & 1) == 1 for b in range(5)]

    def pick(level, base):
        if level < 0:
            row = table[base // 2 : base // 2 + 1, (base % 2) * LANES : (base % 2 + 1) * LANES]
            return jnp.take_along_axis(jnp.broadcast_to(row, (8, LANES)), lane, axis=1)
        low = pick(level - 1, base)
        high = pick(level - 1, base + (1 << level))
        return jnp.where(bits[level], high, low)

    return pick(4, 0)


def edge_lookup(rows, column):
    lane = column & (LANES - 1)
    right = ((column >> 7) & 1) == 1

    def read(k):
        return jnp.take_along_axis(jnp.broadcast_to(rows[k], (8, LANES)), lane, axis=1)

    return jnp.where(
        column >= COLS, jnp.where(right, read(3), read(2)), jnp.where(right, read(1), read(0))
    )


def spread(row, count):
    piece = jnp.broadcast_to(row.astype(F32), (16, LANES)).astype(BF16)
    return jnp.concatenate([piece] * (count // 16), 0)


def numbers(count):
    return lax.broadcasted_iota(jnp.int32, (count, LANES), 0).astype(F32).astype(BF16)


def scatter_sum(index, value):
    zero, one = jnp.zeros((), BF16), jnp.ones((), BF16)
    lefts, rights = [], []
    for j in range(BLOCKS):
        i, v = index(j), value(j)
        line = ((i >> 7) & 1) * 16 + (i >> 8)
        head = v.astype(BF16).astype(F32)
        here = spread(line, 32) == numbers(32)
        lefts.append(
            jnp.concatenate(
                [
                    jnp.where(here, spread(head, 32), zero),
                    jnp.where(here, spread(v - head, 32), zero),
                ],
                0,
            )
        )
        rights.append(jnp.where(spread(i & (LANES - 1), LANES) == numbers(LANES), one, zero))
    left = jnp.concatenate(lefts, 1)
    right = jnp.concatenate(rights, 1)
    return lax.dot_general(left, right, (((1,), (1,)), ((), ())), preferred_element_type=F32)


def halves(total):
    both = total[0:32] + total[32:64]
    return jnp.concatenate([both[0:16], both[16:32]], axis=1)


def kernel(
    state,
    coeff,
    vertical,
    send_cell,
    marine_slot,
    weight,
    out,
    own,
    rate,
    table,
    codes,
    weights,
    edge_out,
    edges,
    merged,
    values,
    rows_out,
    rows_in,
    total,
    weight_sum,
    win_rhs,
    win_diag,
    win_code,
    load_sem,
    edge_send,
    edge_recv,
    row_send,
    row_recv,
    rhs_send,
    rhs_recv,
    win_send,
    win_recv,
):
    model = lax.axis_index("comp")
    tile = lax.axis_index("tile")
    turn = lax.rem(tile, 4) // 2

    def at(offset):
        return lax.rem(tile + offset + TILES, TILES)

    def copy_to(source, target, send, recv, comp, piece):
        return pltpu.make_async_remote_copy(
            src_ref=source,
            dst_ref=target,
            send_sem=send,
            recv_sem=recv,
            device_id=(comp, piece),
            device_id_type=MESH,
        )

    def load(source, target, k):
        return pltpu.make_async_copy(source, target, load_sem.at[k])

    def greet(partners):
        for comp, piece in partners:
            pl.semaphore_signal(
                pltpu.get_barrier_semaphore(),
                inc=1,
                device_id=(comp, piece),
                device_id_type=MESH,
            )

    def met(count):
        pl.semaphore_wait(pltpu.get_barrier_semaphore(), count)

    def to_ocean(d):
        return copy_to(rows_out.at[d], rows_in.at[d], row_send.at[d], row_recv.at[d], 1, at(d - 4))

    def to_air(d):
        first = pl.ds(0, BLOCKS)
        return copy_to(
            rows_out.at[d, first],
            rows_in.at[d, first],
            row_send.at[d],
            row_recv.at[d],
            0,
            at(4 - d),
        )

    def edge_to_ocean(e):
        return copy_to(edge_out, edges.at[e], edge_send.at[e], edge_recv.at[e], 1, at(4 - e))

    def behind_first(i):
        return lax.rem(11 - 6 * turn + i * (2 * turn - 1) + 8, 8)

    def ahead_first(i):
        return lax.rem(5 + 6 * turn + i * (1 - 2 * turn) + 8, 8)

    def slab(ref, d, q):
        return ref[pl.ds(64 * q + d, 8, stride=8), :]

    @pl.when(model == 0)
    def _():
        loads = [
            load(state.at[0], own, 2),
            load(coeff.at[0], rate, 3),
            load(send_cell, codes, 0),
            load(weight, weights, 1),
        ]
        for item in loads:
            item.start()
        greet([(1, at(4 - e)) for e in range(SPAN + 2)])
        for item in loads[:2]:
            item.wait()
        s = own[...]
        for k, r in enumerate((0, ROWS - 1)):
            for h in range(2):
                edge_out[2 * k + h : 2 * k + h + 1, :] = own[r : r + 1, h * LANES : (h + 1) * LANES]
        row_id = lax.broadcasted_iota(jnp.int32, (ROWS, COLS), 0)
        above = jnp.where(row_id == 0, 0.0, pltpu.roll(s, 1, 0))
        below = jnp.where(row_id == ROWS - 1, 0.0, pltpu.roll(s, ROWS - 1, 0))
        near = above + below + pltpu.roll(s, 1, 1) + pltpu.roll(s, COLS - 1, 1)
        table[...] = rate[...] * (s + 0.2 * (near - 4.0 * s))
        side_rates = [
            0.2 * rate[r : r + 1, h * LANES : (h + 1) * LANES] for r in (0, ROWS - 1) for h in (0, 1)
        ]
        for item in loads[2:]:
            item.wait()
        for m, (d, e) in enumerate(MERGED):
            for q in range(4):
                part = slice(8 * q, 8 * q + 8)
                cell = slab(codes, d, q)
                if e is not None:
                    cell = cell + reverse_tile(slab(codes, e, 3 - q))
                merged[m, part, :] = cell
                found = lookup(table, cell)
                row = cell >> 8
                column = (cell & (COLS - 1)) + jnp.where(row == ROWS - 1, COLS, 0)
                gain = jnp.where(
                    (row == 0) | (row == ROWS - 1), edge_lookup(side_rates, column), 0.0
                )
                place = column.astype(F32)
                w = slab(weights, d, q)
                rows_out[d, 8 * q : 8 * q + 8, :] = w * found
                rows_out[d, 32 + 8 * q : 40 + 8 * q, :] = w * gain
                rows_out[d, 64 + 8 * q : 72 + 8 * q, :] = place
                if e is not None:
                    p = 3 - q
                    x = slab(weights, e, p)
                    rows_out[e, 8 * p : 8 * p + 8, :] = x * reverse_tile(found)
                    rows_out[e, 32 + 8 * p : 40 + 8 * p, :] = x * reverse_tile(gain)
                    rows_out[e, 64 + 8 * p : 72 + 8 * p, :] = reverse_tile(place)
                    w = w + reverse_tile(x)
                values[m, part, :] = w
        met(SPAN + 2)
        for e in range(SPAN + 2):
            edge_to_ocean(e).start()
        for i in range(SPAN):
            to_ocean(behind_first(i)).start()
        weight_sum[...] = jnp.zeros_like(weight_sum)
        total[...] = jnp.zeros_like(total)

        @pl.loop(0, len(MERGED))
        def _(m):
            weight_sum[...] += scatter_sum(
                lambda j: merged[m, j : j + 1, :], lambda j: values[m, j : j + 1, :]
            )

        share = 1.0 / halves(weight_sum[...])
        order = (3, 4, 1, 0, 2)
        for m, n in zip(order, order[::-1]):

            def either(x, y):
                return x + turn * (y - x)

            d = either(MERGED[m][0], MERGED[n][0])
            to_air(d).wait_recv()
            pair = MERGED[m][1] is not None
            if pair:
                e = either(MERGED[m][1], MERGED[n][1])
                to_air(e).wait_recv()
            for q in range(4):
                v = slab(weights, d, q) * rows_in[d, 8 * q : 8 * q + 8, :]
                if pair:
                    p = 3 - q
                    v = v + reverse_tile(slab(weights, e, p) * rows_in[e, 8 * p : 8 * p + 8, :])
                values[0, 8 * q : 8 * q + 8, :] = v
            which = either(m, n)
            total[...] += scatter_sum(
                lambda j: merged[which, j : j + 1, :], lambda j: values[0, j : j + 1, :]
            )
        out[...] = halves(total[...]) * share
        for e in range(SPAN + 2):
            edge_to_ocean(e).wait_send()
        for d in range(SPAN):
            to_ocean(d).wait_send()

    @pl.when(model == 1)
    def _():
        mine = pl.ds(OWN, ROWS)
        loads = [
            load(marine_slot, codes, 0),
            load(state.at[0], own, 1),
            load(coeff.at[0], win_diag.at[mine], 2),
            load(vertical, win_code.at[mine], 3),
        ]
        for item in loads:
            item.start()
        greet(
            [(0, at(e - 4)) for e in range(SPAN + 2)]
            + [(1, at(1)), (1, at(-1)), (1, at(2)), (1, at(-2))]
        )

        def to_windows(source, target, send, recv):
            return [
                copy_to(
                    source(first, rows),
                    target.at[pl.ds(place, rows)],
                    send.at[k],
                    recv.at[k],
                    1,
                    at(offset),
                )
                for k, (offset, first, rows, place) in enumerate(
                    (
                        (1, 0, 16, OWN - 16),
                        (-1, 0, 16, OWN + 16),
                        (2, 8, 8, OWN - 24),
                        (-2, 0, 8, OWN + 32),
                    )
                )
            ]

        ahead = to_windows(
            lambda first, rows: coeff.at[0, pl.ds(first, rows)],
            win_diag,
            win_send.at[0],
            win_recv.at[0],
        ) + to_windows(
            lambda first, rows: vertical.at[pl.ds(first, rows)],
            win_code,
            win_send.at[1],
            win_recv.at[1],
        )
        total[...] = jnp.zeros_like(total)
        met(SPAN + 6)
        for item in ahead:
            item.start()
        for item in loads:
            item.wait()

        def edges_here(slots):
            for e in slots:
                edge_to_ocean(e).wait_recv()

        @pl.when(turn == 0)
        def _():
            edges_here(range(4, 10))

        @pl.when(turn == 1)
        def _():
            edges_here(range(0, 5))

        @pl.loop(0, SPAN)
        def _(i):
            d = behind_first(i)

            @pl.when((turn == 0) & (i == 4))
            def _():
                edges_here(range(0, 4))

            @pl.when((turn == 1) & (i == 3))
            def _():
                edges_here(range(5, 10))

            to_ocean(d).wait_recv()
            above = edges.at[7 - d]
            below = edges.at[9 - d]
            sides = [above[2:3, :], above[3:4, :], below[0:1, :], below[1:2, :]]
            for q in range(4):
                column = rows_in[d, 64 + 8 * q : 72 + 8 * q, :].astype(jnp.int32)
                values[0, 8 * q : 8 * q + 8, :] = rows_in[d, 8 * q : 8 * q + 8, :] + rows_in[
                    d, 32 + 8 * q : 40 + 8 * q, :
                ] * edge_lookup(sides, column)
            total[...] += scatter_sum(
                lambda j: codes[pl.ds(8 * j + d, 1), :], lambda j: values[0, j : j + 1, :]
            )

        source = halves(total[...])
        win_rhs[mine, :] = source + own[...]
        sides = to_windows(
            lambda first, rows: win_rhs.at[pl.ds(OWN + first, rows)], win_rhs, rhs_send, rhs_recv
        )
        for item in sides:
            item.start()
        for item in ahead + sides:
            item.wait_recv()

        def sweeps(eta, count, margin):
            rows = WINDOW - 2 * margin
            part = pl.ds(margin, rows)
            skip = (eta.shape[0] - rows) // 2
            code = win_code[part, :]
            far = code >= 3
            side = code - jnp.where(far, 3, 0)
            from_up = pltpu.roll(side, rows - 1, 0)
            from_down = pltpu.roll(side, 1, 0)
            scale = 1.0 / (win_diag[part, :] + 3.0)
            rhs = win_rhs[part, :]

            def one(_, x):
                left = pltpu.roll(x, 1, 1)
                right = pltpu.roll(x, COLS - 1, 1)
                up = jnp.where(from_up == 0, left, jnp.where(from_up == 1, x, right))
                down = jnp.where(from_down == 0, left, jnp.where(from_down == 1, x, right))
                third = jnp.where(far, pltpu.roll(down, rows - 1, 0), pltpu.roll(up, 1, 0))
                return (rhs + (left + right + third)) * scale

            return lax.fori_loop(0, count, one, eta[skip : skip + rows])

        eta = win_rhs[...] / (win_diag[...] + 3.0)
        eta = sweeps(eta, 3, 0)
        eta = sweeps(eta, 8, 8)
        eta = sweeps(eta, 8, 16)
        eta = eta[8:24]
        table[...] = own[...] + 0.5 * eta - 0.25 * source

        @pl.loop(0, SPAN)
        def _(i):
            d = ahead_first(i)
            for q in range(4):
                rows_out[d, 8 * q : 8 * q + 8, :] = lookup(table, slab(codes, d, q))
            to_air(d).start()

        out[...] = eta
        for item in ahead + sides:
            item.wait_send()
        for d in range(SPAN):
            to_air(d).wait_send()


def shards(state, coeff, vertical, send_cell, incoming_marine_slot, remap_weight):
    def blocks(x):
        return x.reshape(SPAN, BLOCKS, LANES).transpose(1, 0, 2).reshape(SPAN * BLOCKS, LANES)

    anywhere = pl.BlockSpec(memory_space=pltpu.HBM)
    grid = pltpu.VMEM((ROWS, COLS), F32)
    dma = pltpu.SemaphoreType.DMA
    result = pl.pallas_call(
        kernel,
        out_shape=jax.ShapeDtypeStruct((ROWS, COLS), F32),
        in_specs=[anywhere] * 6,
        out_specs=pl.BlockSpec(memory_space=pltpu.VMEM),
        scratch_shapes=[
            grid,
            grid,
            grid,
            pltpu.VMEM((SPAN * BLOCKS, LANES), jnp.int32),
            pltpu.VMEM((SPAN * BLOCKS, LANES), F32),
            pltpu.VMEM((8, LANES), F32),
            pltpu.VMEM((SPAN + 2, 8, LANES), F32),
            pltpu.VMEM((len(MERGED), BLOCKS, LANES), jnp.int32),
            pltpu.VMEM((len(MERGED), BLOCKS, LANES), F32),
            pltpu.VMEM((SPAN, 3 * BLOCKS, LANES), F32),
            pltpu.VMEM((SPAN, 3 * BLOCKS, LANES), F32),
            pltpu.VMEM((64, LANES), F32),
            pltpu.VMEM((64, LANES), F32),
            pltpu.VMEM((WINDOW, COLS), F32),
            pltpu.VMEM((WINDOW, COLS), F32),
            pltpu.VMEM((WINDOW, COLS), jnp.int32),
            dma((4,)),
            dma((SPAN + 2,)),
            dma((SPAN + 2,)),
            dma((SPAN,)),
            dma((SPAN,)),
            dma((4,)),
            dma((4,)),
            dma((2, 4)),
            dma((2, 4)),
        ],
        compiler_params=pltpu.CompilerParams(
            collective_id=0, has_side_effects=True, vmem_limit_bytes=40 << 20
        ),
    )(
        *(
            pltpu.with_memory_space_constraint(x, pltpu.HBM)
            for x in (
                state,
                coeff,
                vertical,
                blocks(send_cell),
                blocks(incoming_marine_slot),
                blocks(remap_weight),
            )
        )
    )
    return result[None]


def solution(mesh):
    in_specs = (
        P("comp", "tile", None),
        P("comp", "tile", None),
        P("tile", None),
        P(("comp", "tile"), None),
        P(("comp", "tile"), None),
        P(("comp", "tile"), None),
    )
    out_specs = P("comp", "tile", None)
    return jax.shard_map(shards, mesh=mesh, in_specs=in_specs, out_specs=out_specs, check_vma=False)
```

```python
import functools

import jax
import jax.numpy as jnp
from jax import lax
from jax.experimental import pallas as pl
from jax.experimental.pallas import tpu as pltpu
from jax.sharding import PartitionSpec as P

SPAN = 8
SWEEPS = 20
TILES = 64
ROWS = 16
COLS = 256
CELLS = ROWS * COLS
LANES = 128
BLOCKS = CELLS // LANES
MERGED = ((0, 1), (2, 4), (3, None), (5, None), (6, 7))
OWN = 24
INNER = 2 * COLS
WINDOW = 64
FIRST = 4
DEPTH = 7
MESH = pl.DeviceIdType.MESH
F32 = jnp.float32
BF16 = jnp.bfloat16


def reverse_tile(x):
    row = 7 - lax.broadcasted_iota(jnp.int32, (8, LANES), 0)
    lane = LANES - 1 - lax.broadcasted_iota(jnp.int32, (8, LANES), 1)
    return jnp.take_along_axis(jnp.take_along_axis(x, row, axis=0), lane, axis=1)


def by_half(cell):
    return (cell >> 7) & 1, cell & (LANES - 1)


def by_parity(cell):
    return cell & 1, (cell >> 1) & (LANES - 1)


def lookup(table, index, split=by_half):
    half, lane = split(index)
    bits = [half == 1] + [((index >> (8 + b)) & 1) == 1 for b in range(4)]

    def pick(level, base):
        if level < 0:
            row = table[base // 2 : base // 2 + 1, (base % 2) * LANES : (base % 2 + 1) * LANES]
            return jnp.take_along_axis(jnp.broadcast_to(row, (8, LANES)), lane, axis=1)
        low = pick(level - 1, base)
        high = pick(level - 1, base + (1 << level))
        return jnp.where(bits[level], high, low)

    return pick(4, 0)


def edge_lookup(rows, column):
    lane = column & (LANES - 1)
    right = ((column >> 7) & 1) == 1

    def read(k):
        return jnp.take_along_axis(jnp.broadcast_to(rows[k], (8, LANES)), lane, axis=1)

    return jnp.where(
        column >= COLS, jnp.where(right, read(3), read(2)), jnp.where(right, read(1), read(0))
    )


def spread(row, count):
    piece = jnp.broadcast_to(row.astype(F32), (16, LANES)).astype(BF16)
    return jnp.concatenate([piece] * (count // 16), 0)


def numbers(count):
    return lax.broadcasted_iota(jnp.int32, (count, LANES), 0).astype(F32).astype(BF16)


def scatter_sum(index, value, split=by_half):
    zero, one = jnp.zeros((), BF16), jnp.ones((), BF16)
    lefts, rights = [], []
    for j in range(BLOCKS):
        i, v = index(j), value(j)
        half, lane = split(i)
        line = half * 16 + (i >> 8)
        head = v.astype(BF16).astype(F32)
        here = spread(line, 32) == numbers(32)
        lefts.append(
            jnp.concatenate(
                [
                    jnp.where(here, spread(head, 32), zero),
                    jnp.where(here, spread(v - head, 32), zero),
                ],
                0,
            )
        )
        rights.append(jnp.where(spread(lane, LANES) == numbers(LANES), one, zero))
    left = jnp.concatenate(lefts, 1)
    right = jnp.concatenate(rights, 1)
    return lax.dot_general(left, right, (((1,), (1,)), ((), ())), preferred_element_type=F32)


def even_odd(ref, first):
    parts = [ref[first : first + 8, h * LANES : (h + 1) * LANES] for h in (0, 1)]
    lane = lax.broadcasted_iota(jnp.int32, (8, LANES), 1)
    found = []
    for odd in (0, 1):
        place = (2 * lane + odd) & (LANES - 1)
        left, right = (jnp.take_along_axis(x, place, axis=1) for x in parts)
        found.append(jnp.where(lane < LANES // 2, left, right))
    return found


def interleaved(even, odd):
    lane = lax.broadcasted_iota(jnp.int32, (8, LANES), 1)
    parts = []
    for h in (0, 1):
        place = (lane >> 1) + h * (LANES // 2)
        x, y = (jnp.take_along_axis(part, place, axis=1) for part in (even, odd))
        parts.append(jnp.where((lane & 1) == 0, x, y))
    return jnp.concatenate(parts, axis=1)


def halves(total):
    both = total[0:32] + total[32:64]
    return jnp.concatenate([both[0:16], both[16:32]], axis=1)


def kernel(
    state,
    coeff,
    vertical,
    send_cell,
    marine_slot,
    weight,
    out,
    own,
    rate,
    table,
    codes,
    weights,
    edge_out,
    edges,
    merged,
    values,
    rows_out,
    rows_in,
    total,
    weight_sum,
    win_rhs,
    win_diag,
    win_code,
    scale,
    turns,
    tile_first,
    tile_scale,
    tile_far,
    tile_side,
    load_sem,
    edge_send,
    edge_recv,
    row_send,
    row_recv,
    rhs_send,
    rhs_recv,
    win_send,
    win_recv,
):
    model = lax.axis_index("comp")
    tile = lax.axis_index("tile")
    line = lax.rem(tile, 16) // 4
    is_first = (3 - line) // 3
    is_last = line // 3

    def at(offset):
        return lax.rem(tile + offset + TILES, TILES)

    def copy_to(source, target, send, recv, comp, piece):
        return pltpu.make_async_remote_copy(
            src_ref=source,
            dst_ref=target,
            send_sem=send,
            recv_sem=recv,
            device_id=(comp, piece),
            device_id_type=MESH,
        )

    def load(source, target, k):
        return pltpu.make_async_copy(source, target, load_sem.at[k])

    def greet(partners):
        for comp, piece in partners:
            pl.semaphore_signal(
                pltpu.get_barrier_semaphore(),
                inc=1,
                device_id=(comp, piece),
                device_id_type=MESH,
            )

    def met(count):
        pl.semaphore_wait(pltpu.get_barrier_semaphore(), count)

    def to_ocean(d):
        return copy_to(rows_out.at[d], rows_in.at[d], row_send.at[d], row_recv.at[d], 1, at(d - 4))

    def to_air(d):
        first = pl.ds(0, BLOCKS)
        return copy_to(
            rows_out.at[d, first],
            rows_in.at[d, first],
            row_send.at[d],
            row_recv.at[d],
            0,
            at(4 - d),
        )

    def edge_to_ocean(e):
        return copy_to(edge_out, edges.at[e], edge_send.at[e], edge_recv.at[e], 1, at(4 - e))

    def in_order(first, middle, last):
        first, middle, last = (
            sum(d * 8**i for i, d in enumerate(order)) for order in (first, middle, last)
        )
        return middle + is_first * (first - middle) + is_last * (last - middle)

    row_order = in_order(
        (3, 2, 1, 0, 4, 5, 6, 7), (3, 5, 2, 6, 1, 7, 0, 4), (5, 6, 7, 4, 0, 3, 2, 1)
    )

    def for_each(order, body):
        def step(i, rest):
            body(i, lax.rem(rest, 8))
            return rest // 8

        lax.fori_loop(0, SPAN, step, order)

    def slab(ref, d, q):
        return ref[pl.ds(64 * q + d, 8, stride=8), :]

    @pl.when(model == 0)
    def _():
        loads = [
            load(state.at[0], own, 2),
            load(coeff.at[0], rate, 3),
            load(send_cell, codes, 0),
            load(weight, weights, 1),
        ]
        for item in loads:
            item.start()
        greet([(1, at(4 - e)) for e in range(SPAN + 2)])
        for item in loads[:2]:
            item.wait()
        s = own[...]
        near = s + pltpu.roll(s, 1, 1) + pltpu.roll(s, COLS - 1, 1)
        above, below = pltpu.roll(s, 1, 0), pltpu.roll(s, ROWS - 1, 0)
        table[...] = 0.2 * rate[...] * (near + above + below)
        for k, (r, part) in enumerate(((0, near + below), (ROWS - 1, near + above))):
            for h in range(2):
                at_side = slice(h * LANES, (h + 1) * LANES)
                edge_out[2 * k + h : 2 * k + h + 1, :] = s[r : r + 1, at_side]
                edge_out[4 + 2 * k + h : 5 + 2 * k + h, :] = part[r : r + 1, at_side]
        side_rates = [
            0.2 * rate[r : r + 1, h * LANES : (h + 1) * LANES] for r in (0, ROWS - 1) for h in (0, 1)
        ]
        for item in loads[2:]:
            item.wait()
        for m, (d, e) in enumerate(MERGED):
            for q in range(4):
                part = slice(8 * q, 8 * q + 8)
                cell = slab(codes, d, q)
                if e is not None:
                    cell = cell + reverse_tile(slab(codes, e, 3 - q))
                merged[m, part, :] = cell
                row = cell >> 8
                column = (cell & (COLS - 1)) + jnp.where(row == ROWS - 1, COLS, 0)
                outer = (row == 0) | (row == ROWS - 1)
                found = jnp.where(outer, edge_lookup(side_rates, column), lookup(table, cell))
                place = jnp.where(outer, column, INNER).astype(F32)
                w = slab(weights, d, q)
                rows_out[d, part, :] = w * found
                rows_out[d, 32 + 8 * q : 40 + 8 * q, :] = place
                if e is not None:
                    p = 3 - q
                    x = slab(weights, e, p)
                    rows_out[e, 8 * p : 8 * p + 8, :] = x * reverse_tile(found)
                    rows_out[e, 32 + 8 * p : 40 + 8 * p, :] = reverse_tile(place)
                    w = w + reverse_tile(x)
                values[m, part, :] = w
        met(SPAN + 2)
        for e in range(SPAN + 2):
            edge_to_ocean(e).start()
        for_each(row_order, lambda i, d: to_ocean(d).start())
        weight_sum[...] = jnp.zeros_like(weight_sum)
        total[...] = jnp.zeros_like(total)

        @pl.loop(0, len(MERGED))
        def _(m):
            weight_sum[...] += scatter_sum(
                lambda j: merged[m, j : j + 1, :], lambda j: values[m, j : j + 1, :]
            )

        share = 1.0 / halves(weight_sum[...])
        order = (2, 0, 1, 4, 3)
        for m, n in zip(order, order[::-1]):

            def either(x, y):
                return x + is_first * (y - x)

            d = either(MERGED[m][0], MERGED[n][0])
            to_air(d).wait_recv()
            pair = MERGED[m][1] is not None
            if pair:
                e = either(MERGED[m][1], MERGED[n][1])
                to_air(e).wait_recv()
            for q in range(4):
                v = slab(weights, d, q) * rows_in[d, 8 * q : 8 * q + 8, :]
                if pair:
                    p = 3 - q
                    v = v + reverse_tile(slab(weights, e, p) * rows_in[e, 8 * p : 8 * p + 8, :])
                values[0, 8 * q : 8 * q + 8, :] = v
            which = either(m, n)
            total[...] += scatter_sum(
                lambda j: merged[which, j : j + 1, :], lambda j: values[0, j : j + 1, :]
            )
        out[...] = halves(total[...]) * share
        for e in range(SPAN + 2):
            edge_to_ocean(e).wait_send()
        for d in range(SPAN):
            to_ocean(d).wait_send()

    @pl.when(model == 1)
    def _():
        mine = pl.ds(OWN, ROWS)
        loads = [
            load(marine_slot, codes, 0),
            load(state.at[0], own, 1),
            load(coeff.at[0], win_diag.at[mine], 2),
            load(vertical, win_code.at[mine], 3),
        ]
        for item in loads:
            item.start()
        greet(
            [(0, at(e - 4)) for e in range(SPAN + 2)]
            + [(1, at(1)), (1, at(-1)), (1, at(2)), (1, at(-2))]
        )

        def to_windows(source, target, send, recv):
            return [
                copy_to(source(first, rows), target(place, rows), send.at[k], recv.at[k], 1, at(offset))
                for k, (offset, first, rows, place) in enumerate(
                    (
                        (1, 0, 16, OWN - 16),
                        (-1, 0, 16, OWN + 16),
                        (2, 8, 8, OWN - 24),
                        (-2, 0, 8, OWN + 32),
                    )
                )
            ]

        ahead = to_windows(
            lambda first, rows: coeff.at[0, pl.ds(first, rows)],
            lambda place, rows: win_diag.at[pl.ds(place, rows)],
            win_send.at[0],
            win_recv.at[0],
        ) + to_windows(
            lambda first, rows: vertical.at[pl.ds(first, rows)],
            lambda place, rows: win_code.at[pl.ds(place, rows)],
            win_send.at[1],
            win_recv.at[1],
        )
        total[...] = jnp.zeros_like(total)
        met(SPAN + 6)
        for item in ahead:
            item.start()
        for item in loads:
            item.wait()

        def edges_here(slots):
            for e in slots:
                edge_to_ocean(e).wait_recv()

        @pl.when(is_last == 0)
        def _():
            edges_here(range(4, 10))

        @pl.when(is_first == 0)
        def _():
            edges_here(range(0, 4))

        @pl.when(is_last == 1)
        def _():
            edges_here(range(4, 5))

        def take(i, rest):
            @pl.when((is_first == 1) & (i == 2))
            def _():
                edges_here(range(0, 4))

            @pl.when((is_last == 1) & (i == 1))
            def _():
                edges_here(range(5, 10))

            pair = (lax.rem(rest, 8), lax.rem(rest // 8, 8))
            for d in pair:
                to_ocean(d).wait_recv()
            for k, d in enumerate(pair):
                above, here, below = edges.at[7 - d], edges.at[8 - d], edges.at[9 - d]
                sides = [
                    here[4:5, :] + above[2:3, :],
                    here[5:6, :] + above[3:4, :],
                    here[6:7, :] + below[0:1, :],
                    here[7:8, :] + below[1:2, :],
                ]
                for q in range(4):
                    column = rows_in[d, 32 + 8 * q : 40 + 8 * q, :].astype(jnp.int32)
                    factor = jnp.where(column < INNER, edge_lookup(sides, column), 1.0)
                    values[k, 8 * q : 8 * q + 8, :] = rows_in[d, 8 * q : 8 * q + 8, :] * factor
            sums = [
                scatter_sum(
                    lambda j: codes[pl.ds(8 * j + d, 1), :], lambda j: values[k, j : j + 1, :], by_parity
                )
                for k, d in enumerate(pair)
            ]
            total[...] += sums[0] + sums[1]
            return rest // 64

        lax.fori_loop(0, SPAN // 2, take, row_order)
        both = total[0:32] + total[32:64]
        for k in (0, 1):
            for h, x in enumerate(even_odd(own, 8 * k)):
                part = slice(16 * h + 8 * k, 16 * h + 8 * k + 8)
                win_rhs[h, OWN + 8 * k : OWN + 8 * k + 8, :] = both[part] + x
                table[8 * k : 8 * k + 8, h * LANES : (h + 1) * LANES] = x - 0.25 * both[part]
        sides = to_windows(
            lambda first, rows: win_rhs.at[:, pl.ds(OWN + first, rows)],
            lambda place, rows: win_rhs.at[:, pl.ds(place, rows)],
            rhs_send,
            rhs_recv,
        )
        for item in sides:
            item.start()
        for item in ahead:
            item.wait_recv()
        for k in range(WINDOW // 8):
            for h, x in enumerate(even_odd(win_diag, 8 * k)):
                scale[h, 8 * k : 8 * k + 8, :] = 1.0 / (x + 3.0)
            for h, x in enumerate(even_odd(win_code, 8 * k)):
                turns[h, 8 * k : 8 * k + 8, :] = x
        at_tile = [pl.ds(FIRST + i, 8, stride=DEPTH) for i in range(DEPTH)]
        for h in (0, 1):
            for i in range(DEPTH):
                code = turns[h, at_tile[i], :]
                ahead_row = jnp.where(code >= 3, 1, 0)
                tile_far[h, i] = ahead_row
                tile_side[h, i] = code - 3 * ahead_row
                tile_scale[h, i] = scale[h, at_tile[i], :]
        for item in sides:
            item.wait_recv()
        for h in (0, 1):
            for i in range(DEPTH):
                tile_first[h, i] = win_rhs[h, at_tile[i], :] * tile_scale[h, i]

        def sweep(_, eta):
            even, odd = list(eta[:DEPTH]), list(eta[DEPTH:])
            before = [pltpu.roll(x, 1, 1) for x in odd]
            after = [pltpu.roll(x, LANES - 1, 1) for x in even]

            def extended(x):
                return [pltpu.roll(x[-1], 1, 0)] + x + [pltpu.roll(x[0], 7, 0)]

            even, odd, before, after = map(extended, (even, odd, before, after))
            result = []
            for h, (left, middle, right) in enumerate(((before, even, odd), (even, odd, after))):
                for i in range(DEPTH):
                    far = tile_far[h, i] == 1
                    side = tile_side[h, i]
                    x, y, z = (jnp.where(far, v[i + 2], v[i]) for v in (left, middle, right))
                    third = jnp.where(side == 0, x, jnp.where(side == 1, y, z))
                    near = left[i + 1] + right[i + 1] + third
                    result.append(tile_first[h, i] + near * tile_scale[h, i])
            return tuple(result)

        eta = tuple(tile_first[h, i] for h in (0, 1) for i in range(DEPTH))
        eta = lax.fori_loop(0, SWEEPS - 1, sweep, eta)
        for h in (0, 1):
            for i in range(DEPTH):
                scale[h, at_tile[i], :] = eta[DEPTH * h + i]
        mine_eta = [scale[h, OWN : OWN + ROWS, :] for h in (0, 1)]
        table[...] = table[...] + 0.5 * jnp.concatenate(mine_eta, axis=1)
        back = (3, 2, 0, 1, 6, 7, 5, 4)
        rest = in_order((5, 6, 7, 2, 0, 1, 3, 4), back, back)
        for _ in range(SPAN):
            d = lax.rem(rest, 8)
            rest = rest // 8
            for q in range(4):
                rows_out[d, 8 * q : 8 * q + 8, :] = lookup(table, slab(codes, d, q), by_parity)
            to_air(d).start()

        for k in (0, 1):
            rows = slice(8 * k, 8 * k + 8)
            out[rows, :] = interleaved(mine_eta[0][rows], mine_eta[1][rows])
        for item in ahead + sides:
            item.wait_send()
        for d in range(SPAN):
            to_air(d).wait_send()


def shards(state, coeff, vertical, send_cell, incoming_marine_slot, remap_weight):
    def blocks(x):
        return x.reshape(SPAN, BLOCKS, LANES).transpose(1, 0, 2).reshape(SPAN * BLOCKS, LANES)

    anywhere = pl.BlockSpec(memory_space=pltpu.HBM)
    grid = pltpu.VMEM((ROWS, COLS), F32)
    dma = pltpu.SemaphoreType.DMA
    result = pl.pallas_call(
        kernel,
        out_shape=jax.ShapeDtypeStruct((ROWS, COLS), F32),
        in_specs=[anywhere] * 6,
        out_specs=pl.BlockSpec(memory_space=pltpu.VMEM),
        scratch_shapes=[
            grid,
            grid,
            grid,
            pltpu.VMEM((SPAN * BLOCKS, LANES), jnp.int32),
            pltpu.VMEM((SPAN * BLOCKS, LANES), F32),
            pltpu.VMEM((8, LANES), F32),
            pltpu.VMEM((SPAN + 2, 8, LANES), F32),
            pltpu.VMEM((len(MERGED), BLOCKS, LANES), jnp.int32),
            pltpu.VMEM((len(MERGED), BLOCKS, LANES), F32),
            pltpu.VMEM((SPAN, 2 * BLOCKS, LANES), F32),
            pltpu.VMEM((SPAN, 2 * BLOCKS, LANES), F32),
            pltpu.VMEM((64, LANES), F32),
            pltpu.VMEM((64, LANES), F32),
            pltpu.VMEM((2, WINDOW, LANES), F32),
            pltpu.VMEM((WINDOW, COLS), F32),
            pltpu.VMEM((WINDOW, COLS), jnp.int32),
            pltpu.VMEM((2, WINDOW, LANES), F32),
            pltpu.VMEM((2, WINDOW, LANES), jnp.int32),
            pltpu.VMEM((2, DEPTH, 8, LANES), F32),
            pltpu.VMEM((2, DEPTH, 8, LANES), F32),
            pltpu.VMEM((2, DEPTH, 8, LANES), jnp.int32),
            pltpu.VMEM((2, DEPTH, 8, LANES), jnp.int32),
            dma((4,)),
            dma((SPAN + 2,)),
            dma((SPAN + 2,)),
            dma((SPAN,)),
            dma((SPAN,)),
            dma((4,)),
            dma((4,)),
            dma((2, 4)),
            dma((2, 4)),
        ],
        compiler_params=pltpu.CompilerParams(
            collective_id=0, has_side_effects=True, vmem_limit_bytes=40 << 20
        ),
    )(
        *(
            pltpu.with_memory_space_constraint(x, pltpu.HBM)
            for x in (
                state,
                coeff,
                vertical,
                blocks(send_cell),
                blocks(incoming_marine_slot),
                blocks(remap_weight),
            )
        )
    )
    return result[None]


def solution(mesh):
    in_specs = (
        P("comp", "tile", None),
        P("comp", "tile", None),
        P("tile", None),
        P(("comp", "tile"), None),
        P(("comp", "tile"), None),
        P(("comp", "tile"), None),
    )
    out_specs = P("comp", "tile", None)
    return jax.shard_map(shards, mesh=mesh, in_specs=in_specs, out_specs=out_specs, check_vma=False)
```

```python
import functools

import jax
import jax.numpy as jnp
from jax import lax
from jax.experimental import pallas as pl
from jax.experimental.pallas import tpu as pltpu
from jax.sharding import PartitionSpec as P

SPAN = 8
SWEEPS = 20
TILES = 64
ROWS = 16
COLS = 256
CELLS = ROWS * COLS
LANES = 128
BLOCKS = CELLS // LANES
MERGED = ((0, 1), (2, 4), (3, None), (5, None), (6, 7))
OWN = 24
INNER = 2 * COLS
WINDOW = 64
STAGES = ((7, 8), (5, 8), (3, 3))
MESH = pl.DeviceIdType.MESH
F32 = jnp.float32
BF16 = jnp.bfloat16


def reverse_tile(x):
    row = 7 - lax.broadcasted_iota(jnp.int32, (8, LANES), 0)
    lane = LANES - 1 - lax.broadcasted_iota(jnp.int32, (8, LANES), 1)
    return jnp.take_along_axis(jnp.take_along_axis(x, row, axis=0), lane, axis=1)


def by_half(cell):
    return (cell >> 7) & 1, cell & (LANES - 1)


def by_parity(cell):
    return cell & 1, (cell >> 1) & (LANES - 1)


def lookup(table, index, split=by_half):
    half, lane = split(index)
    bits = [half == 1] + [((index >> (8 + b)) & 1) == 1 for b in range(4)]

    def pick(level, base):
        if level < 0:
            row = table[base // 2 : base // 2 + 1, (base % 2) * LANES : (base % 2 + 1) * LANES]
            return jnp.take_along_axis(jnp.broadcast_to(row, (8, LANES)), lane, axis=1)
        low = pick(level - 1, base)
        high = pick(level - 1, base + (1 << level))
        return jnp.where(bits[level], high, low)

    return pick(4, 0)


def edge_lookup(rows, column):
    lane = column & (LANES - 1)
    right = ((column >> 7) & 1) == 1

    def read(k):
        return jnp.take_along_axis(jnp.broadcast_to(rows[k], (8, LANES)), lane, axis=1)

    return jnp.where(
        column >= COLS, jnp.where(right, read(3), read(2)), jnp.where(right, read(1), read(0))
    )


def spread(row, count):
    piece = jnp.broadcast_to(row.astype(F32), (16, LANES)).astype(BF16)
    return jnp.concatenate([piece] * (count // 16), 0)


def numbers(count):
    return lax.broadcasted_iota(jnp.int32, (count, LANES), 0).astype(F32).astype(BF16)


def scatter_sum(index, value, split=by_half):
    zero, one = jnp.zeros((), BF16), jnp.ones((), BF16)
    lefts, rights = [], []
    for j in range(BLOCKS):
        i, v = index(j), value(j)
        half, lane = split(i)
        line = half * 16 + (i >> 8)
        head = v.astype(BF16).astype(F32)
        here = spread(line, 32) == numbers(32)
        lefts.append(
            jnp.concatenate(
                [
                    jnp.where(here, spread(head, 32), zero),
                    jnp.where(here, spread(v - head, 32), zero),
                ],
                0,
            )
        )
        rights.append(jnp.where(spread(lane, LANES) == numbers(LANES), one, zero))
    left = jnp.concatenate(lefts, 1)
    right = jnp.concatenate(rights, 1)
    return lax.dot_general(left, right, (((1,), (1,)), ((), ())), preferred_element_type=F32)


def even_odd(ref, first):
    parts = [ref[first : first + 8, h * LANES : (h + 1) * LANES] for h in (0, 1)]
    lane = lax.broadcasted_iota(jnp.int32, (8, LANES), 1)
    found = []
    for odd in (0, 1):
        place = (2 * lane + odd) & (LANES - 1)
        left, right = (jnp.take_along_axis(x, place, axis=1) for x in parts)
        found.append(jnp.where(lane < LANES // 2, left, right))
    return found


def interleaved(even, odd):
    lane = lax.broadcasted_iota(jnp.int32, (8, LANES), 1)
    parts = []
    for h in (0, 1):
        place = (lane >> 1) + h * (LANES // 2)
        x, y = (jnp.take_along_axis(part, place, axis=1) for part in (even, odd))
        parts.append(jnp.where((lane & 1) == 0, x, y))
    return jnp.concatenate(parts, axis=1)


def halves(total):
    both = total[0:32] + total[32:64]
    return jnp.concatenate([both[0:16], both[16:32]], axis=1)


def kernel(
    state,
    coeff,
    vertical,
    send_cell,
    marine_slot,
    weight,
    out,
    own,
    rate,
    table,
    codes,
    weights,
    edge_out,
    edges,
    merged,
    values,
    rows_out,
    rows_in,
    total,
    weight_sum,
    win_rhs,
    win_diag,
    win_code,
    scale,
    turns,
    tile_first,
    tile_scale,
    tile_far,
    tile_side,
    load_sem,
    edge_send,
    edge_recv,
    row_send,
    row_recv,
    rhs_send,
    rhs_recv,
    win_send,
    win_recv,
):
    model = lax.axis_index("comp")
    tile = lax.axis_index("tile")
    line = lax.rem(tile, 16) // 4
    is_first = (3 - line) // 3
    is_last = line // 3

    def at(offset):
        return lax.rem(tile + offset + TILES, TILES)

    def copy_to(source, target, send, recv, comp, piece):
        return pltpu.make_async_remote_copy(
            src_ref=source,
            dst_ref=target,
            send_sem=send,
            recv_sem=recv,
            device_id=(comp, piece),
            device_id_type=MESH,
        )

    def load(source, target, k):
        return pltpu.make_async_copy(source, target, load_sem.at[k])

    def greet(partners):
        for comp, piece in partners:
            pl.semaphore_signal(
                pltpu.get_barrier_semaphore(),
                inc=1,
                device_id=(comp, piece),
                device_id_type=MESH,
            )

    def met(count):
        pl.semaphore_wait(pltpu.get_barrier_semaphore(), count)

    def to_ocean(d):
        return copy_to(rows_out.at[d], rows_in.at[d], row_send.at[d], row_recv.at[d], 1, at(d - 4))

    def to_air(d):
        first = pl.ds(0, BLOCKS)
        return copy_to(
            rows_out.at[d, first],
            rows_in.at[d, first],
            row_send.at[d],
            row_recv.at[d],
            0,
            at(4 - d),
        )

    def edge_to_ocean(e):
        return copy_to(edge_out, edges.at[e], edge_send.at[e], edge_recv.at[e], 1, at(4 - e))

    def in_order(first, middle, last):
        first, middle, last = (
            sum(d * 8**i for i, d in enumerate(order)) for order in (first, middle, last)
        )
        return middle + is_first * (first - middle) + is_last * (last - middle)

    row_order = in_order(
        (3, 2, 1, 0, 4, 5, 6, 7), (3, 5, 2, 6, 1, 7, 0, 4), (5, 6, 7, 4, 0, 3, 2, 1)
    )

    def for_each(order, body):
        def step(i, rest):
            body(i, lax.rem(rest, 8))
            return rest // 8

        lax.fori_loop(0, SPAN, step, order)

    def slab(ref, d, q):
        return ref[pl.ds(64 * q + d, 8, stride=8), :]

    @pl.when(model == 0)
    def _():
        loads = [
            load(state.at[0], own, 2),
            load(coeff.at[0], rate, 3),
            load(send_cell, codes, 0),
            load(weight, weights, 1),
        ]
        for item in loads:
            item.start()
        greet([(1, at(offset)) for offset in (1, 2, 3, 4, -1, -2, -3, -4, -5, 0)])
        for item in loads[:2]:
            item.wait()
        s = own[...]
        near = s + pltpu.roll(s, 1, 1) + pltpu.roll(s, COLS - 1, 1)
        above, below = pltpu.roll(s, 1, 0), pltpu.roll(s, ROWS - 1, 0)
        table[...] = 0.2 * rate[...] * (near + above + below)
        for k, (r, part) in enumerate(((0, near + below), (ROWS - 1, near + above))):
            for h in range(2):
                at_side = slice(h * LANES, (h + 1) * LANES)
                edge_out[2 * k + h : 2 * k + h + 1, :] = s[r : r + 1, at_side]
                edge_out[4 + 2 * k + h : 5 + 2 * k + h, :] = part[r : r + 1, at_side]
        side_rates = [
            0.2 * rate[r : r + 1, h * LANES : (h + 1) * LANES] for r in (0, ROWS - 1) for h in (0, 1)
        ]
        for item in loads[2:]:
            item.wait()
        for m, (d, e) in enumerate(MERGED):
            for q in range(4):
                part = slice(8 * q, 8 * q + 8)
                cell = slab(codes, d, q)
                if e is not None:
                    cell = cell + reverse_tile(slab(codes, e, 3 - q))
                merged[m, part, :] = cell
                row = cell >> 8
                column = (cell & (COLS - 1)) + jnp.where(row == ROWS - 1, COLS, 0)
                outer = (row == 0) | (row == ROWS - 1)
                found = jnp.where(outer, edge_lookup(side_rates, column), lookup(table, cell))
                place = jnp.where(outer, column, INNER).astype(F32)
                w = slab(weights, d, q)
                rows_out[d, part, :] = w * found
                rows_out[d, 32 + 8 * q : 40 + 8 * q, :] = place
                if e is not None:
                    p = 3 - q
                    x = slab(weights, e, p)
                    rows_out[e, 8 * p : 8 * p + 8, :] = x * reverse_tile(found)
                    rows_out[e, 32 + 8 * p : 40 + 8 * p, :] = reverse_tile(place)
                    w = w + reverse_tile(x)
                values[m, part, :] = w
        met(SPAN + 2)
        for e in range(SPAN + 2):
            edge_to_ocean(e).start()
        for_each(row_order, lambda i, d: to_ocean(d).start())
        weight_sum[...] = jnp.zeros_like(weight_sum)
        total[...] = jnp.zeros_like(total)

        @pl.loop(0, len(MERGED))
        def _(m):
            weight_sum[...] += scatter_sum(
                lambda j: merged[m, j : j + 1, :], lambda j: values[m, j : j + 1, :]
            )

        share = 1.0 / halves(weight_sum[...])
        order = (2, 0, 1, 4, 3)
        steps = list(enumerate(zip(order, order[::-1])))

        def either(x, y):
            return x + is_first * (y - x)

        for group in (steps[:1], steps[1:2], steps[2:]):
            ready = []
            for k, (m, n) in group:
                ends = [
                    either(x, y) for x, y in zip(MERGED[m], MERGED[n]) if x is not None
                ]
                for d in ends:
                    to_air(d).wait_recv()
                ready.append((k, either(m, n), ends))
            for k, _, ends in ready:
                for q in range(4):
                    d, p = ends[0], 3 - q
                    v = slab(weights, d, q) * rows_in[d, 8 * q : 8 * q + 8, :]
                    if len(ends) == 2:
                        e = ends[1]
                        v = v + reverse_tile(slab(weights, e, p) * rows_in[e, 8 * p : 8 * p + 8, :])
                    values[k, 8 * q : 8 * q + 8, :] = v
            for k, which, _ in ready:
                total[...] += scatter_sum(
                    lambda j: merged[which, j : j + 1, :], lambda j: values[k, j : j + 1, :]
                )
        out[...] = halves(total[...]) * share
        for e in range(SPAN + 2):
            edge_to_ocean(e).wait_send()
        for d in range(SPAN):
            to_ocean(d).wait_send()

    @pl.when(model == 1)
    def _():
        mine = pl.ds(OWN, ROWS)
        loads = [
            load(marine_slot, codes, 0),
            load(state.at[0], own, 1),
            load(coeff.at[0], win_diag.at[mine], 2),
            load(vertical, win_code.at[mine], 3),
        ]
        for item in loads:
            item.start()
        greet(
            [(1, at(1)), (1, at(2))]
            + [(0, at(offset)) for offset in (1, 2, 3, 4, 5, -1, -2, -3, -4, 0)]
            + [(1, at(-1)), (1, at(-2))]
        )

        def to_windows(source, target, send, recv):
            return [
                copy_to(source(first, rows), target(place, rows), send.at[k], recv.at[k], 1, at(offset))
                for k, (offset, first, rows, place) in enumerate(
                    (
                        (1, 0, 16, OWN - 16),
                        (-1, 0, 16, OWN + 16),
                        (2, 8, 8, OWN - 24),
                        (-2, 0, 8, OWN + 32),
                    )
                )
            ]

        ahead = to_windows(
            lambda first, rows: coeff.at[0, pl.ds(first, rows)],
            lambda place, rows: win_diag.at[pl.ds(place, rows)],
            win_send.at[0],
            win_recv.at[0],
        ) + to_windows(
            lambda first, rows: vertical.at[pl.ds(first, rows)],
            lambda place, rows: win_code.at[pl.ds(place, rows)],
            win_send.at[1],
            win_recv.at[1],
        )
        total[...] = jnp.zeros_like(total)
        met(SPAN + 6)
        for item in ahead:
            item.start()
        for item in loads:
            item.wait()

        def edges_here(slots):
            for e in slots:
                edge_to_ocean(e).wait_recv()

        @pl.when(is_last == 0)
        def _():
            edges_here(range(4, 10))

        @pl.when(is_first == 0)
        def _():
            edges_here(range(0, 4))

        @pl.when(is_last == 1)
        def _():
            edges_here(range(4, 5))

        def take(i, rest):
            @pl.when((is_first == 1) & (i == 2))
            def _():
                edges_here(range(0, 4))

            @pl.when((is_last == 1) & (i == 1))
            def _():
                edges_here(range(5, 10))

            pair = (lax.rem(rest, 8), lax.rem(rest // 8, 8))
            for d in pair:
                to_ocean(d).wait_recv()
            for k, d in enumerate(pair):
                above, here, below = edges.at[7 - d], edges.at[8 - d], edges.at[9 - d]
                sides = [
                    here[4:5, :] + above[2:3, :],
                    here[5:6, :] + above[3:4, :],
                    here[6:7, :] + below[0:1, :],
                    here[7:8, :] + below[1:2, :],
                ]
                for q in range(4):
                    column = rows_in[d, 32 + 8 * q : 40 + 8 * q, :].astype(jnp.int32)
                    factor = jnp.where(column < INNER, edge_lookup(sides, column), 1.0)
                    values[k, 8 * q : 8 * q + 8, :] = rows_in[d, 8 * q : 8 * q + 8, :] * factor
            sums = [
                scatter_sum(
                    lambda j: codes[pl.ds(8 * j + d, 1), :], lambda j: values[k, j : j + 1, :], by_parity
                )
                for k, d in enumerate(pair)
            ]
            total[...] += sums[0] + sums[1]
            return rest // 64

        lax.fori_loop(0, SPAN // 2, take, row_order)
        both = total[0:32] + total[32:64]
        for k in (0, 1):
            for h, x in enumerate(even_odd(own, 8 * k)):
                part = slice(16 * h + 8 * k, 16 * h + 8 * k + 8)
                win_rhs[h, OWN + 8 * k : OWN + 8 * k + 8, :] = both[part] + x
                table[8 * k : 8 * k + 8, h * LANES : (h + 1) * LANES] = x - 0.25 * both[part]
        sides = to_windows(
            lambda first, rows: win_rhs.at[:, pl.ds(OWN + first, rows)],
            lambda place, rows: win_rhs.at[:, pl.ds(place, rows)],
            rhs_send,
            rhs_recv,
        )
        for item in sides:
            item.start()
        for item in ahead:
            item.wait_recv()
        for k in range(WINDOW // 8):
            for h, x in enumerate(even_odd(win_diag, 8 * k)):
                scale[h, 8 * k : 8 * k + 8, :] = 1.0 / (x + 3.0)
            for h, x in enumerate(even_odd(win_code, 8 * k)):
                turns[h, 8 * k : 8 * k + 8, :] = x
        def tiles(depth):
            return [pl.ds(OWN + ROWS // 2 - 4 * depth + i, 8, stride=depth) for i in range(depth)]

        for n, (depth, _) in enumerate(STAGES):
            for h in (0, 1):
                for i, rows in enumerate(tiles(depth)):
                    code = turns[h, rows, :]
                    ahead_row = jnp.where(code >= 3, 1, 0)
                    tile_far[n, h, i] = ahead_row
                    tile_side[n, h, i] = code - 3 * ahead_row
                    tile_scale[n, h, i] = scale[h, rows, :]
        for item in sides:
            item.wait_recv()
        for n, (depth, _) in enumerate(STAGES):
            for h in (0, 1):
                for i, rows in enumerate(tiles(depth)):
                    tile_first[n, h, i] = win_rhs[h, rows, :] * tile_scale[n, h, i]

        def sweep(n, eta):
            depth = STAGES[n][0]
            even, odd = list(eta[:depth]), list(eta[depth:])
            before = [pltpu.roll(x, 1, 1) for x in odd]
            after = [pltpu.roll(x, LANES - 1, 1) for x in even]

            def extended(x):
                return [pltpu.roll(x[-1], 1, 0)] + x + [pltpu.roll(x[0], 7, 0)]

            even, odd, before, after = map(extended, (even, odd, before, after))
            result = []
            for h, (left, middle, right) in enumerate(((before, even, odd), (even, odd, after))):
                for i in range(depth):
                    far = tile_far[n, h, i] == 1
                    side = tile_side[n, h, i]
                    x, y, z = (jnp.where(far, v[i + 2], v[i]) for v in (left, middle, right))
                    third = jnp.where(side == 0, x, jnp.where(side == 1, y, z))
                    near = left[i + 1] + right[i + 1] + third
                    result.append(tile_first[n, h, i] + near * tile_scale[n, h, i])
            return tuple(result)

        for n, (depth, count) in enumerate(STAGES):
            if n == 0:
                eta = tuple(tile_first[0, h, i] for h in (0, 1) for i in range(depth))
            else:
                eta = tuple(scale[h, rows, :] for h in (0, 1) for rows in tiles(depth))
            for _ in range(count):
                eta = sweep(n, eta)
            for h in (0, 1):
                for i, rows in enumerate(tiles(depth)):
                    scale[h, rows, :] = eta[depth * h + i]
        mine_eta = [scale[h, OWN : OWN + ROWS, :] for h in (0, 1)]
        table[...] = table[...] + 0.5 * jnp.concatenate(mine_eta, axis=1)
        start = is_last * (3 - lax.rem(tile, 4))
        back = (3, 2, 1, 0, 6, 7, 5, 4)
        rest = in_order((5, 6, 7, 2, 0, 1, 3, 4), (3, 2, 0, 1, 6, 7, 5, 4), back)
        for k in range(SPAN):
            d = lax.rem(rest, 8)
            rest = rest // 8
            if k < 4:
                d = d + is_last * (lax.rem(d - start + 4, 4) - d)
            for q in range(4):
                rows_out[d, 8 * q : 8 * q + 8, :] = lookup(table, slab(codes, d, q), by_parity)
            to_air(d).start()

        for k in (0, 1):
            rows = slice(8 * k, 8 * k + 8)
            out[rows, :] = interleaved(mine_eta[0][rows], mine_eta[1][rows])
        for item in ahead + sides:
            item.wait_send()
        for d in range(SPAN):
            to_air(d).wait_send()


def shards(state, coeff, vertical, send_cell, incoming_marine_slot, remap_weight):
    def blocks(x):
        return x.reshape(SPAN, BLOCKS, LANES).transpose(1, 0, 2).reshape(SPAN * BLOCKS, LANES)

    anywhere = pl.BlockSpec(memory_space=pltpu.HBM)
    grid = pltpu.VMEM((ROWS, COLS), F32)
    dma = pltpu.SemaphoreType.DMA
    result = pl.pallas_call(
        kernel,
        out_shape=jax.ShapeDtypeStruct((ROWS, COLS), F32),
        in_specs=[anywhere] * 6,
        out_specs=pl.BlockSpec(memory_space=pltpu.VMEM),
        scratch_shapes=[
            grid,
            grid,
            grid,
            pltpu.VMEM((SPAN * BLOCKS, LANES), jnp.int32),
            pltpu.VMEM((SPAN * BLOCKS, LANES), F32),
            pltpu.VMEM((8, LANES), F32),
            pltpu.VMEM((SPAN + 2, 8, LANES), F32),
            pltpu.VMEM((len(MERGED), BLOCKS, LANES), jnp.int32),
            pltpu.VMEM((len(MERGED), BLOCKS, LANES), F32),
            pltpu.VMEM((SPAN, 2 * BLOCKS, LANES), F32),
            pltpu.VMEM((SPAN, 2 * BLOCKS, LANES), F32),
            pltpu.VMEM((64, LANES), F32),
            pltpu.VMEM((64, LANES), F32),
            pltpu.VMEM((2, WINDOW, LANES), F32),
            pltpu.VMEM((WINDOW, COLS), F32),
            pltpu.VMEM((WINDOW, COLS), jnp.int32),
            pltpu.VMEM((2, WINDOW, LANES), F32),
            pltpu.VMEM((2, WINDOW, LANES), jnp.int32),
            pltpu.VMEM((len(STAGES), 2, STAGES[0][0], 8, LANES), F32),
            pltpu.VMEM((len(STAGES), 2, STAGES[0][0], 8, LANES), F32),
            pltpu.VMEM((len(STAGES), 2, STAGES[0][0], 8, LANES), jnp.int32),
            pltpu.VMEM((len(STAGES), 2, STAGES[0][0], 8, LANES), jnp.int32),
            dma((4,)),
            dma((SPAN + 2,)),
            dma((SPAN + 2,)),
            dma((SPAN,)),
            dma((SPAN,)),
            dma((4,)),
            dma((4,)),
            dma((2, 4)),
            dma((2, 4)),
        ],
        compiler_params=pltpu.CompilerParams(
            collective_id=0, has_side_effects=True, vmem_limit_bytes=40 << 20
        ),
    )(
        *(
            pltpu.with_memory_space_constraint(x, pltpu.HBM)
            for x in (
                state,
                coeff,
                vertical,
                blocks(send_cell),
                blocks(incoming_marine_slot),
                blocks(remap_weight),
            )
        )
    )
    return result[None]


def solution(mesh):
    in_specs = (
        P("comp", "tile", None),
        P("comp", "tile", None),
        P("tile", None),
        P(("comp", "tile"), None),
        P(("comp", "tile"), None),
        P(("comp", "tile"), None),
    )
    out_specs = P("comp", "tile", None)
    return jax.shard_map(shards, mesh=mesh, in_specs=in_specs, out_specs=out_specs, check_vma=False)
```

```python
import functools

import jax
import jax.numpy as jnp
from jax import lax
from jax.experimental import pallas as pl
from jax.experimental.pallas import tpu as pltpu
from jax.sharding import PartitionSpec as P

SPAN = 8
SWEEPS = 20
TILES = 64
ROWS = 16
COLS = 256
CELLS = ROWS * COLS
LANES = 128
BLOCKS = CELLS // LANES
MERGED = ((0, 1), (2, 4), (3, None), (5, None), (6, 7))
OWN = 24
INNER = 2 * COLS
WINDOW = 64
STAGES = ((7, 8), (5, 8), (3, 3))
MESH = pl.DeviceIdType.MESH
F32 = jnp.float32
BF16 = jnp.bfloat16


def reverse_tile(x):
    row = 7 - lax.broadcasted_iota(jnp.int32, (8, LANES), 0)
    lane = LANES - 1 - lax.broadcasted_iota(jnp.int32, (8, LANES), 1)
    return jnp.take_along_axis(jnp.take_along_axis(x, row, axis=0), lane, axis=1)


def by_half(cell):
    return (cell >> 7) & 1, cell & (LANES - 1)


def by_parity(cell):
    return cell & 1, (cell >> 1) & (LANES - 1)


def lookup(table, index, split=by_half):
    half, lane = split(index)
    bits = [half == 1] + [((index >> (8 + b)) & 1) == 1 for b in range(4)]

    def pick(level, base):
        if level < 0:
            row = table[base // 2 : base // 2 + 1, (base % 2) * LANES : (base % 2 + 1) * LANES]
            return jnp.take_along_axis(jnp.broadcast_to(row, (8, LANES)), lane, axis=1)
        low = pick(level - 1, base)
        high = pick(level - 1, base + (1 << level))
        return jnp.where(bits[level], high, low)

    return pick(4, 0)


def edge_lookup(rows, column):
    lane = column & (LANES - 1)
    right = ((column >> 7) & 1) == 1

    def read(k):
        return jnp.take_along_axis(jnp.broadcast_to(rows[k], (8, LANES)), lane, axis=1)

    return jnp.where(
        column >= COLS, jnp.where(right, read(3), read(2)), jnp.where(right, read(1), read(0))
    )


def spread(row, count):
    piece = jnp.broadcast_to(row.astype(F32), (16, LANES)).astype(BF16)
    return jnp.concatenate([piece] * (count // 16), 0)


def numbers(count):
    return lax.broadcasted_iota(jnp.int32, (count, LANES), 0).astype(F32).astype(BF16)


def scatter_sum(index, value, split=by_half):
    zero, one = jnp.zeros((), BF16), jnp.ones((), BF16)
    lefts, rights = [], []
    for j in range(BLOCKS):
        i, v = index(j), value(j)
        half, lane = split(i)
        line = half * 16 + (i >> 8)
        head = v.astype(BF16).astype(F32)
        here = spread(line, 32) == numbers(32)
        lefts.append(
            jnp.concatenate(
                [
                    jnp.where(here, spread(head, 32), zero),
                    jnp.where(here, spread(v - head, 32), zero),
                ],
                0,
            )
        )
        rights.append(jnp.where(spread(lane, LANES) == numbers(LANES), one, zero))
    left = jnp.concatenate(lefts, 1)
    right = jnp.concatenate(rights, 1)
    return lax.dot_general(left, right, (((1,), (1,)), ((), ())), preferred_element_type=F32)


def even_odd(ref, first):
    parts = [ref[first : first + 8, h * LANES : (h + 1) * LANES] for h in (0, 1)]
    lane = lax.broadcasted_iota(jnp.int32, (8, LANES), 1)
    found = []
    for odd in (0, 1):
        place = (2 * lane + odd) & (LANES - 1)
        left, right = (jnp.take_along_axis(x, place, axis=1) for x in parts)
        found.append(jnp.where(lane < LANES // 2, left, right))
    return found


def interleaved(even, odd):
    lane = lax.broadcasted_iota(jnp.int32, (8, LANES), 1)
    parts = []
    for h in (0, 1):
        place = (lane >> 1) + h * (LANES // 2)
        x, y = (jnp.take_along_axis(part, place, axis=1) for part in (even, odd))
        parts.append(jnp.where((lane & 1) == 0, x, y))
    return jnp.concatenate(parts, axis=1)


def halves(total):
    both = total[0:32] + total[32:64]
    return jnp.concatenate([both[0:16], both[16:32]], axis=1)


def kernel(
    state,
    coeff,
    vertical,
    send_cell,
    marine_slot,
    weight,
    out,
    own,
    rate,
    table,
    codes,
    weights,
    edge_out,
    edges,
    merged,
    values,
    rows_out,
    rows_in,
    total,
    weight_sum,
    win_rhs,
    win_diag,
    win_code,
    scale,
    turns,
    tile_first,
    tile_scale,
    tile_far,
    tile_side,
    load_sem,
    edge_send,
    edge_recv,
    row_send,
    row_recv,
    rhs_send,
    rhs_recv,
    win_send,
    win_recv,
):
    model = lax.axis_index("comp")
    tile = lax.axis_index("tile")
    line = lax.rem(tile, 16) // 4
    is_first = (3 - line) // 3
    is_last = line // 3

    def at(offset):
        return lax.rem(tile + offset + TILES, TILES)

    def copy_to(source, target, send, recv, comp, piece):
        return pltpu.make_async_remote_copy(
            src_ref=source,
            dst_ref=target,
            send_sem=send,
            recv_sem=recv,
            device_id=(comp, piece),
            device_id_type=MESH,
        )

    def load(source, target, k):
        return pltpu.make_async_copy(source, target, load_sem.at[k])

    def greet(partners):
        for comp, piece in partners:
            pl.semaphore_signal(
                pltpu.get_barrier_semaphore(),
                inc=1,
                device_id=(comp, piece),
                device_id_type=MESH,
            )

    def met(count):
        pl.semaphore_wait(pltpu.get_barrier_semaphore(), count)

    def to_ocean(d):
        return copy_to(rows_out.at[d], rows_in.at[d], row_send.at[d], row_recv.at[d], 1, at(d - 4))

    def to_air(d):
        first = pl.ds(0, BLOCKS)
        return copy_to(
            rows_out.at[d, first],
            rows_in.at[d, first],
            row_send.at[d],
            row_recv.at[d],
            0,
            at(4 - d),
        )

    def edge_to_ocean(e):
        return copy_to(edge_out, edges.at[e], edge_send.at[e], edge_recv.at[e], 1, at(4 - e))

    def in_order(first, middle, last):
        first, middle, last = (
            sum(d * 8**i for i, d in enumerate(order)) for order in (first, middle, last)
        )
        return middle + is_first * (first - middle) + is_last * (last - middle)

    row_order = in_order(
        (3, 2, 1, 0, 4, 5, 6, 7), (5, 6, 7, 2, 4, 3, 0, 1), (5, 6, 7, 4, 0, 3, 2, 1)
    )

    def slab(ref, d, q):
        return ref[pl.ds(64 * q + d, 8, stride=8), :]

    @pl.when(model == 0)
    def _():
        loads = [
            load(state.at[0], own, 2),
            load(coeff.at[0], rate, 3),
            load(send_cell, codes, 0),
            load(weight, weights, 1),
        ]
        for item in loads:
            item.start()
        greet([(1, at(offset)) for offset in (1, 2, 3, 4, -1, -2, -3, -4, -5, 0)])
        for item in loads[:2]:
            item.wait()
        s = own[...]
        near = s + pltpu.roll(s, 1, 1) + pltpu.roll(s, COLS - 1, 1)
        above, below = pltpu.roll(s, 1, 0), pltpu.roll(s, ROWS - 1, 0)
        table[...] = 0.2 * rate[...] * (near + above + below)
        for k, (r, part) in enumerate(((0, near + below), (ROWS - 1, near + above))):
            for h in range(2):
                at_side = slice(h * LANES, (h + 1) * LANES)
                edge_out[2 * k + h : 2 * k + h + 1, :] = s[r : r + 1, at_side]
                edge_out[4 + 2 * k + h : 5 + 2 * k + h, :] = part[r : r + 1, at_side]
        side_rates = [
            0.2 * rate[r : r + 1, h * LANES : (h + 1) * LANES] for r in (0, ROWS - 1) for h in (0, 1)
        ]
        for item in loads[2:]:
            item.wait()
        def either(x, y):
            return x + is_first * (y - x)

        def prepare(m, d, e):
            for q in range(4):
                part = slice(8 * q, 8 * q + 8)
                cell = slab(codes, d, q)
                if e is not None:
                    cell = cell + reverse_tile(slab(codes, e, 3 - q))
                merged[m, part, :] = cell
                row = cell >> 8
                column = (cell & (COLS - 1)) + jnp.where(row == ROWS - 1, COLS, 0)
                outer = (row == 0) | (row == ROWS - 1)
                found = jnp.where(outer, edge_lookup(side_rates, column), lookup(table, cell))
                place = jnp.where(outer, column, INNER).astype(F32)
                w = slab(weights, d, q)
                rows_out[d, part, :] = w * found
                rows_out[d, 32 + 8 * q : 40 + 8 * q, :] = place
                if e is not None:
                    p = 3 - q
                    x = slab(weights, e, p)
                    rows_out[e, 8 * p : 8 * p + 8, :] = x * reverse_tile(found)
                    rows_out[e, 32 + 8 * p : 40 + 8 * p, :] = reverse_tile(place)
                    w = w + reverse_tile(x)
                values[m, part, :] = w

        def prepare_all(pairs):
            for x, y in pairs:
                prepare(
                    either(x, y),
                    either(MERGED[x][0], MERGED[y][0]),
                    None if MERGED[x][1] is None else either(MERGED[x][1], MERGED[y][1]),
                )

        order = list(zip((3, 4, 1, 2, 0), (2, 1, 0, 3, 4)))
        sent = (5, 6, 7, 2, 4, 3, 0, 1)
        rest = in_order((3, 2, 1, 0, 4, 5, 6, 7), sent, sent)
        prepare_all(order[:3])
        met(SPAN + 2)
        for e in range(SPAN + 2):
            edge_to_ocean(e).start()
        for k in range(SPAN):
            if k == 5:
                prepare_all(order[3:])
            to_ocean(lax.rem(rest, 8)).start()
            rest = rest // 8
        weight_sum[...] = jnp.zeros_like(weight_sum)
        total[...] = jnp.zeros_like(total)

        @pl.loop(0, len(MERGED))
        def _(m):
            weight_sum[...] += scatter_sum(
                lambda j: merged[m, j : j + 1, :], lambda j: values[m, j : j + 1, :]
            )

        share = 1.0 / halves(weight_sum[...])
        order = (2, 0, 1, 4, 3)
        steps = list(enumerate(zip(order, order[::-1])))

        for group in (steps[:1], steps[1:2], steps[2:]):
            ready = []
            for k, (m, n) in group:
                ends = [
                    either(x, y) for x, y in zip(MERGED[m], MERGED[n]) if x is not None
                ]
                for d in ends:
                    to_air(d).wait_recv()
                ready.append((k, either(m, n), ends))
            for k, _, ends in ready:
                for q in range(4):
                    d, p = ends[0], 3 - q
                    v = slab(weights, d, q) * rows_in[d, 8 * q : 8 * q + 8, :]
                    if len(ends) == 2:
                        e = ends[1]
                        v = v + reverse_tile(slab(weights, e, p) * rows_in[e, 8 * p : 8 * p + 8, :])
                    values[k, 8 * q : 8 * q + 8, :] = v
            for k, which, _ in ready:
                total[...] += scatter_sum(
                    lambda j: merged[which, j : j + 1, :], lambda j: values[k, j : j + 1, :]
                )
        out[...] = halves(total[...]) * share
        for e in range(SPAN + 2):
            edge_to_ocean(e).wait_send()
        for d in range(SPAN):
            to_ocean(d).wait_send()

    @pl.when(model == 1)
    def _():
        mine = pl.ds(OWN, ROWS)
        loads = [
            load(marine_slot, codes, 0),
            load(state.at[0], own, 1),
            load(coeff.at[0], win_diag.at[mine], 2),
            load(vertical, win_code.at[mine], 3),
        ]
        for item in loads:
            item.start()
        greet(
            [(1, at(1)), (1, at(2))]
            + [(0, at(offset)) for offset in (1, 2, 3, 4, 5, -1, -2, -3, -4, 0)]
            + [(1, at(-1)), (1, at(-2))]
        )

        def to_windows(source, target, send, recv):
            return [
                copy_to(source(first, rows), target(place, rows), send.at[k], recv.at[k], 1, at(offset))
                for k, (offset, first, rows, place) in enumerate(
                    (
                        (1, 0, 16, OWN - 16),
                        (-1, 0, 16, OWN + 16),
                        (2, 8, 8, OWN - 24),
                        (-2, 0, 8, OWN + 32),
                    )
                )
            ]

        ahead = to_windows(
            lambda first, rows: coeff.at[0, pl.ds(first, rows)],
            lambda place, rows: win_diag.at[pl.ds(place, rows)],
            win_send.at[0],
            win_recv.at[0],
        ) + to_windows(
            lambda first, rows: vertical.at[pl.ds(first, rows)],
            lambda place, rows: win_code.at[pl.ds(place, rows)],
            win_send.at[1],
            win_recv.at[1],
        )
        total[...] = jnp.zeros_like(total)
        met(SPAN + 6)
        for item in ahead:
            item.start()
        for item in loads:
            item.wait()

        def edges_here(slots):
            for e in slots:
                edge_to_ocean(e).wait_recv()

        @pl.when(is_last == 0)
        def _():
            edges_here(range(4, 10))

        @pl.when(is_first == 0)
        def _():
            edges_here(range(0, 4))

        @pl.when(is_last == 1)
        def _():
            edges_here(range(4, 5))

        def take(i, rest):
            @pl.when((is_first == 1) & (i == 2))
            def _():
                edges_here(range(0, 4))

            @pl.when((is_last == 1) & (i == 1))
            def _():
                edges_here(range(5, 10))

            pair = (lax.rem(rest, 8), lax.rem(rest // 8, 8))
            for d in pair:
                to_ocean(d).wait_recv()
            for k, d in enumerate(pair):
                above, here, below = edges.at[7 - d], edges.at[8 - d], edges.at[9 - d]
                sides = [
                    here[4:5, :] + above[2:3, :],
                    here[5:6, :] + above[3:4, :],
                    here[6:7, :] + below[0:1, :],
                    here[7:8, :] + below[1:2, :],
                ]
                for q in range(4):
                    column = rows_in[d, 32 + 8 * q : 40 + 8 * q, :].astype(jnp.int32)
                    factor = jnp.where(column < INNER, edge_lookup(sides, column), 1.0)
                    values[k, 8 * q : 8 * q + 8, :] = rows_in[d, 8 * q : 8 * q + 8, :] * factor
            sums = [
                scatter_sum(
                    lambda j: codes[pl.ds(8 * j + d, 1), :], lambda j: values[k, j : j + 1, :], by_parity
                )
                for k, d in enumerate(pair)
            ]
            total[...] += sums[0] + sums[1]
            return rest // 64

        lax.fori_loop(0, SPAN // 2, take, row_order)
        both = total[0:32] + total[32:64]
        for k in (0, 1):
            for h, x in enumerate(even_odd(own, 8 * k)):
                part = slice(16 * h + 8 * k, 16 * h + 8 * k + 8)
                win_rhs[h, OWN + 8 * k : OWN + 8 * k + 8, :] = both[part] + x
                table[8 * k : 8 * k + 8, h * LANES : (h + 1) * LANES] = x - 0.25 * both[part]
        sides = to_windows(
            lambda first, rows: win_rhs.at[:, pl.ds(OWN + first, rows)],
            lambda place, rows: win_rhs.at[:, pl.ds(place, rows)],
            rhs_send,
            rhs_recv,
        )
        for item in sides:
            item.start()
        for item in ahead:
            item.wait_recv()
        for k in range(WINDOW // 8):
            for h, x in enumerate(even_odd(win_diag, 8 * k)):
                scale[h, 8 * k : 8 * k + 8, :] = 1.0 / (x + 3.0)
            for h, x in enumerate(even_odd(win_code, 8 * k)):
                turns[h, 8 * k : 8 * k + 8, :] = x
        def tiles(depth):
            return [pl.ds(OWN + ROWS // 2 - 4 * depth + i, 8, stride=depth) for i in range(depth)]

        for n, (depth, _) in enumerate(STAGES):
            for h in (0, 1):
                for i, rows in enumerate(tiles(depth)):
                    code = turns[h, rows, :]
                    ahead_row = jnp.where(code >= 3, 1, 0)
                    tile_far[n, h, i] = ahead_row
                    tile_side[n, h, i] = code - 3 * ahead_row
                    tile_scale[n, h, i] = scale[h, rows, :]
        for item in sides:
            item.wait_recv()
        for n, (depth, _) in enumerate(STAGES):
            for h in (0, 1):
                for i, rows in enumerate(tiles(depth)):
                    tile_first[n, h, i] = win_rhs[h, rows, :] * tile_scale[n, h, i]

        def sweep(n, eta):
            depth = STAGES[n][0]
            even, odd = list(eta[:depth]), list(eta[depth:])
            before = [pltpu.roll(x, 1, 1) for x in odd]
            after = [pltpu.roll(x, LANES - 1, 1) for x in even]

            def extended(x):
                return [pltpu.roll(x[-1], 1, 0)] + x + [pltpu.roll(x[0], 7, 0)]

            even, odd, before, after = map(extended, (even, odd, before, after))
            result = []
            for h, (left, middle, right) in enumerate(((before, even, odd), (even, odd, after))):
                for i in range(depth):
                    far = tile_far[n, h, i] == 1
                    side = tile_side[n, h, i]
                    x, y, z = (jnp.where(far, v[i + 2], v[i]) for v in (left, middle, right))
                    third = jnp.where(side == 0, x, jnp.where(side == 1, y, z))
                    near = left[i + 1] + right[i + 1] + third
                    result.append(tile_first[n, h, i] + near * tile_scale[n, h, i])
            return tuple(result)

        for n, (depth, count) in enumerate(STAGES):
            if n == 0:
                eta = tuple(tile_first[0, h, i] for h in (0, 1) for i in range(depth))
            else:
                eta = tuple(scale[h, rows, :] for h in (0, 1) for rows in tiles(depth))
            eta = lax.fori_loop(0, count, lambda _, x: sweep(n, x), eta)
            for h in (0, 1):
                for i, rows in enumerate(tiles(depth)):
                    scale[h, rows, :] = eta[depth * h + i]
        mine_eta = [scale[h, OWN : OWN + ROWS, :] for h in (0, 1)]
        table[...] = table[...] + 0.5 * jnp.concatenate(mine_eta, axis=1)
        start = is_last * (3 - lax.rem(tile, 4))
        back = (3, 2, 1, 0, 6, 7, 5, 4)
        rest = in_order((5, 6, 7, 2, 0, 1, 3, 4), (3, 2, 0, 1, 6, 7, 5, 4), back)
        def give(i, rest):
            for k in range(2):
                d = lax.rem(rest, 8)
                rest = rest // 8
                back_turn = is_last * ((SPAN - 1 - (2 * i + k)) // 4)
                d = d + back_turn * (lax.rem(d - start + 4, 4) - d)
                for q in range(4):
                    rows_out[d, 8 * q : 8 * q + 8, :] = lookup(table, slab(codes, d, q), by_parity)
                to_air(d).start()
            return rest

        lax.fori_loop(0, SPAN // 2, give, rest)
        for k in (0, 1):
            rows = slice(8 * k, 8 * k + 8)
            out[rows, :] = interleaved(mine_eta[0][rows], mine_eta[1][rows])
        for item in ahead + sides:
            item.wait_send()
        for d in range(SPAN):
            to_air(d).wait_send()


def shards(state, coeff, vertical, send_cell, incoming_marine_slot, remap_weight):
    def blocks(x):
        return x.reshape(SPAN, BLOCKS, LANES).transpose(1, 0, 2).reshape(SPAN * BLOCKS, LANES)

    anywhere = pl.BlockSpec(memory_space=pltpu.HBM)
    grid = pltpu.VMEM((ROWS, COLS), F32)
    dma = pltpu.SemaphoreType.DMA
    result = pl.pallas_call(
        kernel,
        out_shape=jax.ShapeDtypeStruct((ROWS, COLS), F32),
        in_specs=[anywhere] * 6,
        out_specs=pl.BlockSpec(memory_space=pltpu.VMEM),
        scratch_shapes=[
            grid,
            grid,
            grid,
            pltpu.VMEM((SPAN * BLOCKS, LANES), jnp.int32),
            pltpu.VMEM((SPAN * BLOCKS, LANES), F32),
            pltpu.VMEM((8, LANES), F32),
            pltpu.VMEM((SPAN + 2, 8, LANES), F32),
            pltpu.VMEM((len(MERGED), BLOCKS, LANES), jnp.int32),
            pltpu.VMEM((len(MERGED), BLOCKS, LANES), F32),
            pltpu.VMEM((SPAN, 2 * BLOCKS, LANES), F32),
            pltpu.VMEM((SPAN, 2 * BLOCKS, LANES), F32),
            pltpu.VMEM((64, LANES), F32),
            pltpu.VMEM((64, LANES), F32),
            pltpu.VMEM((2, WINDOW, LANES), F32),
            pltpu.VMEM((WINDOW, COLS), F32),
            pltpu.VMEM((WINDOW, COLS), jnp.int32),
            pltpu.VMEM((2, WINDOW, LANES), F32),
            pltpu.VMEM((2, WINDOW, LANES), jnp.int32),
            pltpu.VMEM((len(STAGES), 2, STAGES[0][0], 8, LANES), F32),
            pltpu.VMEM((len(STAGES), 2, STAGES[0][0], 8, LANES), F32),
            pltpu.VMEM((len(STAGES), 2, STAGES[0][0], 8, LANES), jnp.int32),
            pltpu.VMEM((len(STAGES), 2, STAGES[0][0], 8, LANES), jnp.int32),
            dma((4,)),
            dma((SPAN + 2,)),
            dma((SPAN + 2,)),
            dma((SPAN,)),
            dma((SPAN,)),
            dma((4,)),
            dma((4,)),
            dma((2, 4)),
            dma((2, 4)),
        ],
        compiler_params=pltpu.CompilerParams(
            collective_id=0, has_side_effects=True, vmem_limit_bytes=40 << 20
        ),
    )(
        *(
            pltpu.with_memory_space_constraint(x, pltpu.HBM)
            for x in (
                state,
                coeff,
                vertical,
                blocks(send_cell),
                blocks(incoming_marine_slot),
                blocks(remap_weight),
            )
        )
    )
    return result[None]


def solution(mesh):
    in_specs = (
        P("comp", "tile", None),
        P("comp", "tile", None),
        P("tile", None),
        P(("comp", "tile"), None),
        P(("comp", "tile"), None),
        P(("comp", "tile"), None),
    )
    out_specs = P("comp", "tile", None)
    return jax.shard_map(shards, mesh=mesh, in_specs=in_specs, out_specs=out_specs, check_vma=False)
```

```python
import functools

import jax
import jax.numpy as jnp
from jax import lax
from jax.experimental import pallas as pl
from jax.experimental.pallas import tpu as pltpu
from jax.sharding import PartitionSpec as P

SPAN = 8
SWEEPS = 20
TILES = 64
ROWS = 16
COLS = 256
CELLS = ROWS * COLS
LANES = 128
BLOCKS = CELLS // LANES
MERGED = ((0, 1), (2, 4), (3, None), (5, None), (6, 7))
OWN = 24
INNER = 2 * COLS
WINDOW = 64
STAGES = ((7, 8), (5, 8), (3, 3))
MESH = pl.DeviceIdType.MESH
F32 = jnp.float32
BF16 = jnp.bfloat16


def reverse_tile(x):
    row = 7 - lax.broadcasted_iota(jnp.int32, (8, LANES), 0)
    lane = LANES - 1 - lax.broadcasted_iota(jnp.int32, (8, LANES), 1)
    return jnp.take_along_axis(jnp.take_along_axis(x, row, axis=0), lane, axis=1)


def by_half(cell):
    return (cell >> 7) & 1, cell & (LANES - 1)


def by_parity(cell):
    return cell & 1, (cell >> 1) & (LANES - 1)


def lookup(table, index, split=by_half):
    half, lane = split(index)
    bits = [half == 1] + [((index >> (8 + b)) & 1) == 1 for b in range(4)]

    def pick(level, base):
        if level < 0:
            row = table[base // 2 : base // 2 + 1, (base % 2) * LANES : (base % 2 + 1) * LANES]
            return jnp.take_along_axis(jnp.broadcast_to(row, (8, LANES)), lane, axis=1)
        low = pick(level - 1, base)
        high = pick(level - 1, base + (1 << level))
        return jnp.where(bits[level], high, low)

    return pick(4, 0)


def edge_lookup(rows, column):
    lane = column & (LANES - 1)
    right = ((column >> 7) & 1) == 1

    def read(k):
        return jnp.take_along_axis(jnp.broadcast_to(rows[k], (8, LANES)), lane, axis=1)

    return jnp.where(
        column >= COLS, jnp.where(right, read(3), read(2)), jnp.where(right, read(1), read(0))
    )


def spread(row, count):
    piece = jnp.broadcast_to(row.astype(F32), (16, LANES)).astype(BF16)
    return jnp.concatenate([piece] * (count // 16), 0)


def numbers(count):
    return lax.broadcasted_iota(jnp.int32, (count, LANES), 0).astype(F32).astype(BF16)


def scatter_sum(index, value, split=by_half):
    zero, one = jnp.zeros((), BF16), jnp.ones((), BF16)
    lefts, rights = [], []
    for j in range(BLOCKS):
        i, v = index(j), value(j)
        half, lane = split(i)
        line = half * 16 + (i >> 8)
        head = v.astype(BF16).astype(F32)
        here = spread(line, 32) == numbers(32)
        lefts.append(
            jnp.concatenate(
                [
                    jnp.where(here, spread(head, 32), zero),
                    jnp.where(here, spread(v - head, 32), zero),
                ],
                0,
            )
        )
        rights.append(jnp.where(spread(lane, LANES) == numbers(LANES), one, zero))
    left = jnp.concatenate(lefts, 1)
    right = jnp.concatenate(rights, 1)
    return lax.dot_general(left, right, (((1,), (1,)), ((), ())), preferred_element_type=F32)


def even_odd(ref, first):
    parts = [ref[first : first + 8, h * LANES : (h + 1) * LANES] for h in (0, 1)]
    lane = lax.broadcasted_iota(jnp.int32, (8, LANES), 1)
    found = []
    for odd in (0, 1):
        place = (2 * lane + odd) & (LANES - 1)
        left, right = (jnp.take_along_axis(x, place, axis=1) for x in parts)
        found.append(jnp.where(lane < LANES // 2, left, right))
    return found


def interleaved(even, odd):
    lane = lax.broadcasted_iota(jnp.int32, (8, LANES), 1)
    parts = []
    for h in (0, 1):
        place = (lane >> 1) + h * (LANES // 2)
        x, y = (jnp.take_along_axis(part, place, axis=1) for part in (even, odd))
        parts.append(jnp.where((lane & 1) == 0, x, y))
    return jnp.concatenate(parts, axis=1)


def halves(total):
    both = total[0:32] + total[32:64]
    return jnp.concatenate([both[0:16], both[16:32]], axis=1)


def kernel(
    state,
    coeff,
    vertical,
    send_cell,
    marine_slot,
    weight,
    out,
    own,
    rate,
    table,
    codes,
    weights,
    edge_out,
    edges,
    merged,
    values,
    rows_out,
    rows_in,
    total,
    weight_sum,
    win_rhs,
    win_diag,
    win_code,
    scale,
    turns,
    tile_first,
    tile_scale,
    tile_far,
    tile_side,
    load_sem,
    edge_send,
    edge_recv,
    row_send,
    row_recv,
    rhs_send,
    rhs_recv,
    win_send,
    win_recv,
):
    model = lax.axis_index("comp")
    tile = lax.axis_index("tile")
    line = lax.rem(tile, 16) // 4
    is_first = (3 - line) // 3
    is_last = line // 3

    def at(offset):
        return lax.rem(tile + offset + TILES, TILES)

    def copy_to(source, target, send, recv, comp, piece):
        return pltpu.make_async_remote_copy(
            src_ref=source,
            dst_ref=target,
            send_sem=send,
            recv_sem=recv,
            device_id=(comp, piece),
            device_id_type=MESH,
        )

    def load(source, target, k):
        return pltpu.make_async_copy(source, target, load_sem.at[k])

    def greet(partners):
        for comp, piece in partners:
            pl.semaphore_signal(
                pltpu.get_barrier_semaphore(),
                inc=1,
                device_id=(comp, piece),
                device_id_type=MESH,
            )

    def met(count):
        pl.semaphore_wait(pltpu.get_barrier_semaphore(), count)

    def to_ocean(d):
        return copy_to(rows_out.at[d], rows_in.at[d], row_send.at[d], row_recv.at[d], 1, at(d - 4))

    def to_air(d):
        first = pl.ds(0, BLOCKS)
        return copy_to(
            rows_out.at[d, first],
            rows_in.at[d, first],
            row_send.at[d],
            row_recv.at[d],
            0,
            at(4 - d),
        )

    def edge_to_ocean(e):
        return copy_to(edge_out, edges.at[e], edge_send.at[e], edge_recv.at[e], 1, at(4 - e))

    def in_order(first, middle, last):
        first, middle, last = (
            sum(d * 8**i for i, d in enumerate(order)) for order in (first, middle, last)
        )
        return middle + is_first * (first - middle) + is_last * (last - middle)

    row_order = in_order(
        (3, 2, 1, 0, 4, 5, 6, 7), (5, 6, 7, 2, 4, 3, 0, 1), (5, 6, 7, 4, 0, 3, 2, 1)
    )

    def slab(ref, d, q):
        return ref[pl.ds(64 * q + d, 8, stride=8), :]

    @pl.when(model == 0)
    def _():
        loads = [
            load(state.at[0], own, 2),
            load(coeff.at[0], rate, 3),
            load(send_cell, codes, 0),
            load(weight, weights, 1),
        ]
        for item in loads:
            item.start()
        greet([(1, at(offset)) for offset in (1, 2, 3, 4, -1, -2, -3, -4, -5, 0)])
        for item in loads[:2]:
            item.wait()
        s = own[...]
        near = s + pltpu.roll(s, 1, 1) + pltpu.roll(s, COLS - 1, 1)
        above, below = pltpu.roll(s, 1, 0), pltpu.roll(s, ROWS - 1, 0)
        table[...] = 0.2 * rate[...] * (near + above + below)
        for k, (r, part) in enumerate(((0, near + below), (ROWS - 1, near + above))):
            for h in range(2):
                at_side = slice(h * LANES, (h + 1) * LANES)
                edge_out[2 * k + h : 2 * k + h + 1, :] = s[r : r + 1, at_side]
                edge_out[4 + 2 * k + h : 5 + 2 * k + h, :] = part[r : r + 1, at_side]
        side_rates = [
            0.2 * rate[r : r + 1, h * LANES : (h + 1) * LANES] for r in (0, ROWS - 1) for h in (0, 1)
        ]
        for item in loads[2:]:
            item.wait()
        def either(x, y):
            return x + is_first * (y - x)

        def prepare(m, d, e):
            for q in range(4):
                part = slice(8 * q, 8 * q + 8)
                cell = slab(codes, d, q)
                if e is not None:
                    cell = cell + reverse_tile(slab(codes, e, 3 - q))
                merged[m, part, :] = cell
                row = cell >> 8
                column = (cell & (COLS - 1)) + jnp.where(row == ROWS - 1, COLS, 0)
                outer = (row == 0) | (row == ROWS - 1)
                found = jnp.where(outer, edge_lookup(side_rates, column), lookup(table, cell))
                place = jnp.where(outer, column, INNER).astype(F32)
                w = slab(weights, d, q)
                rows_out[d, part, :] = w * found
                rows_out[d, 32 + 8 * q : 40 + 8 * q, :] = place
                if e is not None:
                    p = 3 - q
                    x = slab(weights, e, p)
                    rows_out[e, 8 * p : 8 * p + 8, :] = x * reverse_tile(found)
                    rows_out[e, 32 + 8 * p : 40 + 8 * p, :] = reverse_tile(place)
                    w = w + reverse_tile(x)
                values[m, part, :] = w

        def prepare_all(pairs):
            for x, y in pairs:
                prepare(
                    either(x, y),
                    either(MERGED[x][0], MERGED[y][0]),
                    None if MERGED[x][1] is None else either(MERGED[x][1], MERGED[y][1]),
                )

        order = list(zip((3, 4, 1, 2, 0), (2, 1, 0, 3, 4)))
        sent = (5, 6, 7, 2, 4, 3, 0, 1)
        rest = in_order((3, 2, 1, 0, 4, 5, 6, 7), sent, sent)
        prepare_all(order[:3])
        met(SPAN + 2)
        for e in range(SPAN + 2):
            edge_to_ocean(e).start()
        for k in range(SPAN):
            if k == 5:
                prepare_all(order[3:])
            to_ocean(lax.rem(rest, 8)).start()
            rest = rest // 8
        weight_sum[...] = jnp.zeros_like(weight_sum)
        total[...] = jnp.zeros_like(total)

        @pl.loop(0, len(MERGED))
        def _(m):
            weight_sum[...] += scatter_sum(
                lambda j: merged[m, j : j + 1, :], lambda j: values[m, j : j + 1, :]
            )

        share = 1.0 / halves(weight_sum[...])
        order = (2, 0, 1, 4, 3)
        steps = list(enumerate(zip(order, order[::-1])))

        for group in (steps[:2], steps[2:]):
            ready = []
            for k, (m, n) in group:
                ends = [
                    either(x, y) for x, y in zip(MERGED[m], MERGED[n]) if x is not None
                ]
                for d in ends:
                    to_air(d).wait_recv()
                ready.append((k, either(m, n), ends))
            for k, _, ends in ready:
                for q in range(4):
                    d, p = ends[0], 3 - q
                    v = slab(weights, d, q) * rows_in[d, 8 * q : 8 * q + 8, :]
                    if len(ends) == 2:
                        e = ends[1]
                        v = v + reverse_tile(slab(weights, e, p) * rows_in[e, 8 * p : 8 * p + 8, :])
                    values[k, 8 * q : 8 * q + 8, :] = v
            sums = [
                scatter_sum(lambda j: merged[which, j : j + 1, :], lambda j: values[k, j : j + 1, :])
                for k, which, _ in ready
            ]
            total[...] += sum(sums[1:], sums[0])
        out[...] = halves(total[...]) * share
        for e in range(SPAN + 2):
            edge_to_ocean(e).wait_send()
        for d in range(SPAN):
            to_ocean(d).wait_send()

    @pl.when(model == 1)
    def _():
        mine = pl.ds(OWN, ROWS)
        loads = [
            load(marine_slot, codes, 0),
            load(state.at[0], own, 1),
            load(coeff.at[0], win_diag.at[mine], 2),
            load(vertical, win_code.at[mine], 3),
        ]
        for item in loads:
            item.start()
        greet(
            [(1, at(1)), (1, at(2))]
            + [(0, at(offset)) for offset in (1, 2, 3, 4, 5, -1, -2, -3, -4, 0)]
            + [(1, at(-1)), (1, at(-2))]
        )

        def to_windows(source, target, send, recv):
            return [
                copy_to(source(first, rows), target(place, rows), send.at[k], recv.at[k], 1, at(offset))
                for k, (offset, first, rows, place) in enumerate(
                    (
                        (1, 0, 16, OWN - 16),
                        (-1, 0, 16, OWN + 16),
                        (2, 8, 8, OWN - 24),
                        (-2, 0, 8, OWN + 32),
                    )
                )
            ]

        ahead = to_windows(
            lambda first, rows: coeff.at[0, pl.ds(first, rows)],
            lambda place, rows: win_diag.at[pl.ds(place, rows)],
            win_send.at[0],
            win_recv.at[0],
        ) + to_windows(
            lambda first, rows: vertical.at[pl.ds(first, rows)],
            lambda place, rows: win_code.at[pl.ds(place, rows)],
            win_send.at[1],
            win_recv.at[1],
        )
        total[...] = jnp.zeros_like(total)
        met(SPAN + 6)
        for item in ahead:
            item.start()
        for item in loads:
            item.wait()

        def edges_here(slots):
            for e in slots:
                edge_to_ocean(e).wait_recv()

        @pl.when(is_last == 0)
        def _():
            edges_here(range(4, 10))

        @pl.when(is_first == 0)
        def _():
            edges_here(range(0, 4))

        @pl.when(is_last == 1)
        def _():
            edges_here(range(4, 5))

        def take(i, rest):
            @pl.when((is_first == 1) & (i == 2))
            def _():
                edges_here(range(0, 4))

            @pl.when((is_last == 1) & (i == 1))
            def _():
                edges_here(range(5, 10))

            pair = (lax.rem(rest, 8), lax.rem(rest // 8, 8))
            for d in pair:
                to_ocean(d).wait_recv()
            for k, d in enumerate(pair):
                above, here, below = edges.at[7 - d], edges.at[8 - d], edges.at[9 - d]
                sides = [
                    here[4:5, :] + above[2:3, :],
                    here[5:6, :] + above[3:4, :],
                    here[6:7, :] + below[0:1, :],
                    here[7:8, :] + below[1:2, :],
                ]
                for q in range(4):
                    column = rows_in[d, 32 + 8 * q : 40 + 8 * q, :].astype(jnp.int32)
                    factor = jnp.where(column < INNER, edge_lookup(sides, column), 1.0)
                    values[k, 8 * q : 8 * q + 8, :] = rows_in[d, 8 * q : 8 * q + 8, :] * factor
            sums = [
                scatter_sum(
                    lambda j: codes[pl.ds(8 * j + d, 1), :], lambda j: values[k, j : j + 1, :], by_parity
                )
                for k, d in enumerate(pair)
            ]
            total[...] += sums[0] + sums[1]
            return rest // 64

        lax.fori_loop(0, SPAN // 2, take, row_order)
        both = total[0:32] + total[32:64]
        for k in (0, 1):
            for h, x in enumerate(even_odd(own, 8 * k)):
                part = slice(16 * h + 8 * k, 16 * h + 8 * k + 8)
                win_rhs[h, OWN + 8 * k : OWN + 8 * k + 8, :] = both[part] + x
                table[8 * k : 8 * k + 8, h * LANES : (h + 1) * LANES] = x - 0.25 * both[part]
        sides = to_windows(
            lambda first, rows: win_rhs.at[:, pl.ds(OWN + first, rows)],
            lambda place, rows: win_rhs.at[:, pl.ds(place, rows)],
            rhs_send,
            rhs_recv,
        )
        for item in sides:
            item.start()
        for item in ahead:
            item.wait_recv()
        for k in range(WINDOW // 8):
            for h, x in enumerate(even_odd(win_diag, 8 * k)):
                scale[h, 8 * k : 8 * k + 8, :] = 1.0 / (x + 3.0)
            for h, x in enumerate(even_odd(win_code, 8 * k)):
                turns[h, 8 * k : 8 * k + 8, :] = x
        def tiles(depth):
            return [pl.ds(OWN + ROWS // 2 - 4 * depth + i, 8, stride=depth) for i in range(depth)]

        for n, (depth, _) in enumerate(STAGES):
            for h in (0, 1):
                for i, rows in enumerate(tiles(depth)):
                    code = turns[h, rows, :]
                    ahead_row = jnp.where(code >= 3, 1, 0)
                    tile_far[n, h, i] = ahead_row
                    tile_side[n, h, i] = code - 3 * ahead_row
                    tile_scale[n, h, i] = scale[h, rows, :]
        for item in sides:
            item.wait_recv()
        for n, (depth, _) in enumerate(STAGES):
            for h in (0, 1):
                for i, rows in enumerate(tiles(depth)):
                    tile_first[n, h, i] = win_rhs[h, rows, :] * tile_scale[n, h, i]

        def sweep(n, eta):
            depth = STAGES[n][0]
            even, odd = list(eta[:depth]), list(eta[depth:])
            before = [pltpu.roll(x, 1, 1) for x in odd]
            after = [pltpu.roll(x, LANES - 1, 1) for x in even]

            def extended(x):
                return [pltpu.roll(x[-1], 1, 0)] + x + [pltpu.roll(x[0], 7, 0)]

            even, odd, before, after = map(extended, (even, odd, before, after))
            result = []
            for h, (left, middle, right) in enumerate(((before, even, odd), (even, odd, after))):
                for i in range(depth):
                    far = tile_far[n, h, i] == 1
                    side = tile_side[n, h, i]
                    x, y, z = (jnp.where(far, v[i + 2], v[i]) for v in (left, middle, right))
                    third = jnp.where(side == 0, x, jnp.where(side == 1, y, z))
                    near = left[i + 1] + right[i + 1] + third
                    result.append(tile_first[n, h, i] + near * tile_scale[n, h, i])
            return tuple(result)

        for n, (depth, count) in enumerate(STAGES):
            if n == 0:
                eta = tuple(tile_first[0, h, i] for h in (0, 1) for i in range(depth))
            else:
                eta = tuple(scale[h, rows, :] for h in (0, 1) for rows in tiles(depth))
            eta = lax.fori_loop(0, count, lambda _, x: sweep(n, x), eta)
            for h in (0, 1):
                for i, rows in enumerate(tiles(depth)):
                    scale[h, rows, :] = eta[depth * h + i]
        mine_eta = [scale[h, OWN : OWN + ROWS, :] for h in (0, 1)]
        table[...] = table[...] + 0.5 * jnp.concatenate(mine_eta, axis=1)
        start = is_last * (3 - lax.rem(tile, 4))
        back = (3, 2, 1, 0, 6, 7, 5, 4)
        rest = in_order((5, 6, 7, 2, 0, 1, 3, 4), (3, 2, 0, 1, 6, 7, 5, 4), back)
        def give(i, rest):
            for k in range(2):
                d = lax.rem(rest, 8)
                rest = rest // 8
                back_turn = is_last * ((SPAN - 1 - (2 * i + k)) // 4)
                d = d + back_turn * (lax.rem(d - start + 4, 4) - d)
                for q in range(4):
                    rows_out[d, 8 * q : 8 * q + 8, :] = lookup(table, slab(codes, d, q), by_parity)
                to_air(d).start()
            return rest

        lax.fori_loop(0, SPAN // 2, give, rest)
        for k in (0, 1):
            rows = slice(8 * k, 8 * k + 8)
            out[rows, :] = interleaved(mine_eta[0][rows], mine_eta[1][rows])
        for item in ahead + sides:
            item.wait_send()
        for d in range(SPAN):
            to_air(d).wait_send()


def shards(state, coeff, vertical, send_cell, incoming_marine_slot, remap_weight):
    def blocks(x):
        return x.reshape(SPAN, BLOCKS, LANES).transpose(1, 0, 2).reshape(SPAN * BLOCKS, LANES)

    anywhere = pl.BlockSpec(memory_space=pltpu.HBM)
    grid = pltpu.VMEM((ROWS, COLS), F32)
    dma = pltpu.SemaphoreType.DMA
    result = pl.pallas_call(
        kernel,
        out_shape=jax.ShapeDtypeStruct((ROWS, COLS), F32),
        in_specs=[anywhere] * 6,
        out_specs=pl.BlockSpec(memory_space=pltpu.VMEM),
        scratch_shapes=[
            grid,
            grid,
            grid,
            pltpu.VMEM((SPAN * BLOCKS, LANES), jnp.int32),
            pltpu.VMEM((SPAN * BLOCKS, LANES), F32),
            pltpu.VMEM((8, LANES), F32),
            pltpu.VMEM((SPAN + 2, 8, LANES), F32),
            pltpu.VMEM((len(MERGED), BLOCKS, LANES), jnp.int32),
            pltpu.VMEM((len(MERGED), BLOCKS, LANES), F32),
            pltpu.VMEM((SPAN, 2 * BLOCKS, LANES), F32),
            pltpu.VMEM((SPAN, 2 * BLOCKS, LANES), F32),
            pltpu.VMEM((64, LANES), F32),
            pltpu.VMEM((64, LANES), F32),
            pltpu.VMEM((2, WINDOW, LANES), F32),
            pltpu.VMEM((WINDOW, COLS), F32),
            pltpu.VMEM((WINDOW, COLS), jnp.int32),
            pltpu.VMEM((2, WINDOW, LANES), F32),
            pltpu.VMEM((2, WINDOW, LANES), jnp.int32),
            pltpu.VMEM((len(STAGES), 2, STAGES[0][0], 8, LANES), F32),
            pltpu.VMEM((len(STAGES), 2, STAGES[0][0], 8, LANES), F32),
            pltpu.VMEM((len(STAGES), 2, STAGES[0][0], 8, LANES), jnp.int32),
            pltpu.VMEM((len(STAGES), 2, STAGES[0][0], 8, LANES), jnp.int32),
            dma((4,)),
            dma((SPAN + 2,)),
            dma((SPAN + 2,)),
            dma((SPAN,)),
            dma((SPAN,)),
            dma((4,)),
            dma((4,)),
            dma((2, 4)),
            dma((2, 4)),
        ],
        compiler_params=pltpu.CompilerParams(
            collective_id=0, has_side_effects=True, vmem_limit_bytes=40 << 20
        ),
    )(
        *(
            pltpu.with_memory_space_constraint(x, pltpu.HBM)
            for x in (
                state,
                coeff,
                vertical,
                blocks(send_cell),
                blocks(incoming_marine_slot),
                blocks(remap_weight),
            )
        )
    )
    return result[None]


def solution(mesh):
    in_specs = (
        P("comp", "tile", None),
        P("comp", "tile", None),
        P("tile", None),
        P(("comp", "tile"), None),
        P(("comp", "tile"), None),
        P(("comp", "tile"), None),
    )
    out_specs = P("comp", "tile", None)
    return jax.shard_map(shards, mesh=mesh, in_specs=in_specs, out_specs=out_specs, check_vma=False)
```

```python
import functools

import jax
import jax.numpy as jnp
from jax import lax
from jax.experimental import pallas as pl
from jax.experimental.pallas import tpu as pltpu
from jax.sharding import PartitionSpec as P

SPAN = 8
SWEEPS = 20
TILES = 64
ROWS = 16
COLS = 256
CELLS = ROWS * COLS
LANES = 128
BLOCKS = CELLS // LANES
MERGED = ((0, 1), (2, 4), (3, None), (5, None), (6, 7))
OWN = 24
INNER = 2 * COLS
WINDOW = 64
STAGES = ((7, 8), (5, 8), (3, 3))
MESH = pl.DeviceIdType.MESH
F32 = jnp.float32
BF16 = jnp.bfloat16


def reverse_tile(x):
    row = 7 - lax.broadcasted_iota(jnp.int32, (8, LANES), 0)
    lane = LANES - 1 - lax.broadcasted_iota(jnp.int32, (8, LANES), 1)
    return jnp.take_along_axis(jnp.take_along_axis(x, row, axis=0), lane, axis=1)


def by_half(cell):
    return (cell >> 7) & 1, cell & (LANES - 1)


def by_parity(cell):
    return cell & 1, (cell >> 1) & (LANES - 1)


def lookup(table, index, split=by_half):
    half, lane = split(index)
    bits = [half == 1] + [((index >> (8 + b)) & 1) == 1 for b in range(4)]

    def pick(level, base):
        if level < 0:
            row = table[base // 2 : base // 2 + 1, (base % 2) * LANES : (base % 2 + 1) * LANES]
            return jnp.take_along_axis(jnp.broadcast_to(row, (8, LANES)), lane, axis=1)
        low = pick(level - 1, base)
        high = pick(level - 1, base + (1 << level))
        return jnp.where(bits[level], high, low)

    return pick(4, 0)


def edge_lookup(rows, column):
    lane = column & (LANES - 1)
    right = ((column >> 7) & 1) == 1

    def read(k):
        return jnp.take_along_axis(jnp.broadcast_to(rows[k], (8, LANES)), lane, axis=1)

    return jnp.where(
        column >= COLS, jnp.where(right, read(3), read(2)), jnp.where(right, read(1), read(0))
    )


def spread(row, count):
    piece = jnp.broadcast_to(row.astype(F32), (16, LANES)).astype(BF16)
    return jnp.concatenate([piece] * (count // 16), 0)


def numbers(count):
    return lax.broadcasted_iota(jnp.int32, (count, LANES), 0).astype(F32).astype(BF16)


def scatter_sum(index, value, split=by_half):
    zero, one = jnp.zeros((), BF16), jnp.ones((), BF16)
    lefts, rights = [], []
    for j in range(BLOCKS):
        i, v = index(j), value(j)
        half, lane = split(i)
        line = half * 16 + (i >> 8)
        head = v.astype(BF16).astype(F32)
        here = spread(line, 32) == numbers(32)
        lefts.append(
            jnp.concatenate(
                [
                    jnp.where(here, spread(head, 32), zero),
                    jnp.where(here, spread(v - head, 32), zero),
                ],
                0,
            )
        )
        rights.append(jnp.where(spread(lane, LANES) == numbers(LANES), one, zero))
    left = jnp.concatenate(lefts, 1)
    right = jnp.concatenate(rights, 1)
    return lax.dot_general(left, right, (((1,), (1,)), ((), ())), preferred_element_type=F32)


def even_odd(ref, first):
    parts = [ref[first : first + 8, h * LANES : (h + 1) * LANES] for h in (0, 1)]
    lane = lax.broadcasted_iota(jnp.int32, (8, LANES), 1)
    found = []
    for odd in (0, 1):
        place = (2 * lane + odd) & (LANES - 1)
        left, right = (jnp.take_along_axis(x, place, axis=1) for x in parts)
        found.append(jnp.where(lane < LANES // 2, left, right))
    return found


def interleaved(even, odd):
    lane = lax.broadcasted_iota(jnp.int32, (8, LANES), 1)
    parts = []
    for h in (0, 1):
        place = (lane >> 1) + h * (LANES // 2)
        x, y = (jnp.take_along_axis(part, place, axis=1) for part in (even, odd))
        parts.append(jnp.where((lane & 1) == 0, x, y))
    return jnp.concatenate(parts, axis=1)


def halves(total):
    both = total[0:32] + total[32:64]
    return jnp.concatenate([both[0:16], both[16:32]], axis=1)


def kernel(
    state,
    coeff,
    vertical,
    send_cell,
    marine_slot,
    weight,
    out,
    own,
    rate,
    table,
    codes,
    weights,
    edge_out,
    edges,
    merged,
    values,
    rows_out,
    rows_in,
    total,
    weight_sum,
    win_rhs,
    win_diag,
    win_code,
    scale,
    turns,
    tile_first,
    tile_scale,
    tile_far,
    tile_side,
    load_sem,
    edge_send,
    edge_recv,
    row_send,
    row_recv,
    rhs_send,
    rhs_recv,
    win_send,
    win_recv,
):
    model = lax.axis_index("comp")
    tile = lax.axis_index("tile")
    line = lax.rem(tile, 16) // 4
    is_first = (3 - line) // 3
    is_last = line // 3

    def at(offset):
        return lax.rem(tile + offset + TILES, TILES)

    def copy_to(source, target, send, recv, comp, piece):
        return pltpu.make_async_remote_copy(
            src_ref=source,
            dst_ref=target,
            send_sem=send,
            recv_sem=recv,
            device_id=(comp, piece),
            device_id_type=MESH,
        )

    def load(source, target, k):
        return pltpu.make_async_copy(source, target, load_sem.at[k])

    def greet(partners):
        for comp, piece in partners:
            pl.semaphore_signal(
                pltpu.get_barrier_semaphore(),
                inc=1,
                device_id=(comp, piece),
                device_id_type=MESH,
            )

    def met(count):
        pl.semaphore_wait(pltpu.get_barrier_semaphore(), count)

    def to_ocean(d):
        return copy_to(rows_out.at[d], rows_in.at[d], row_send.at[d], row_recv.at[d], 1, at(d - 4))

    def to_air(d):
        first = pl.ds(0, BLOCKS)
        return copy_to(
            rows_out.at[d, first],
            rows_in.at[d, first],
            row_send.at[d],
            row_recv.at[d],
            0,
            at(4 - d),
        )

    def edge_to_ocean(e):
        return copy_to(edge_out, edges.at[e], edge_send.at[e], edge_recv.at[e], 1, at(4 - e))

    def in_order(first, middle, last):
        first, middle, last = (
            sum(d * 8**i for i, d in enumerate(order)) for order in (first, middle, last)
        )
        return middle + is_first * (first - middle) + is_last * (last - middle)

    row_order = in_order(
        (3, 2, 1, 0, 4, 5, 6, 7), (5, 6, 7, 2, 4, 3, 0, 1), (5, 6, 7, 4, 0, 3, 2, 1)
    )

    def slab(ref, d, q):
        return ref[pl.ds(64 * q + d, 8, stride=8), :]

    @pl.when(model == 0)
    def _():
        loads = [
            load(state.at[0], own, 2),
            load(coeff.at[0], rate, 3),
            load(send_cell, codes, 0),
            load(weight, weights, 1),
        ]
        for item in loads:
            item.start()
        greet([(1, at(offset)) for offset in (1, 2, 3, 4, -1, -2, -3, -4, -5, 0)])
        for item in loads[:2]:
            item.wait()
        s = own[...]
        near = s + pltpu.roll(s, 1, 1) + pltpu.roll(s, COLS - 1, 1)
        above, below = pltpu.roll(s, 1, 0), pltpu.roll(s, ROWS - 1, 0)
        table[...] = 0.2 * rate[...] * (near + above + below)
        for k, (r, part) in enumerate(((0, near + below), (ROWS - 1, near + above))):
            for h in range(2):
                at_side = slice(h * LANES, (h + 1) * LANES)
                edge_out[2 * k + h : 2 * k + h + 1, :] = s[r : r + 1, at_side]
                edge_out[4 + 2 * k + h : 5 + 2 * k + h, :] = part[r : r + 1, at_side]
        side_rates = [
            0.2 * rate[r : r + 1, h * LANES : (h + 1) * LANES] for r in (0, ROWS - 1) for h in (0, 1)
        ]
        for item in loads[2:]:
            item.wait()
        def either(x, y):
            return x + is_first * (y - x)

        def prepare(m, d, e):
            for q in range(4):
                part = slice(8 * q, 8 * q + 8)
                cell = slab(codes, d, q)
                if e is not None:
                    cell = cell + reverse_tile(slab(codes, e, 3 - q))
                merged[m, part, :] = cell
                row = cell >> 8
                column = (cell & (COLS - 1)) + jnp.where(row == ROWS - 1, COLS, 0)
                outer = (row == 0) | (row == ROWS - 1)
                found = jnp.where(outer, edge_lookup(side_rates, column), lookup(table, cell))
                place = jnp.where(outer, column, INNER).astype(F32)
                w = slab(weights, d, q)
                rows_out[d, part, :] = w * found
                rows_out[d, 32 + 8 * q : 40 + 8 * q, :] = place
                if e is not None:
                    p = 3 - q
                    x = slab(weights, e, p)
                    rows_out[e, 8 * p : 8 * p + 8, :] = x * reverse_tile(found)
                    rows_out[e, 32 + 8 * p : 40 + 8 * p, :] = reverse_tile(place)
                    w = w + reverse_tile(x)
                values[m, part, :] = w

        def prepare_all(pairs):
            for x, y in pairs:
                prepare(
                    either(x, y),
                    either(MERGED[x][0], MERGED[y][0]),
                    None if MERGED[x][1] is None else either(MERGED[x][1], MERGED[y][1]),
                )

        order = list(zip((3, 4, 1, 2, 0), (2, 1, 0, 3, 4)))
        sent = (5, 6, 7, 2, 4, 3, 0, 1)
        rest = in_order((3, 2, 1, 0, 4, 5, 6, 7), sent, sent)
        prepare_all(order[:3])
        met(SPAN + 2)
        for e in range(SPAN + 2):
            edge_to_ocean(e).start()
        for k in range(SPAN):
            if k == 5:
                prepare_all(order[3:])
            to_ocean(lax.rem(rest, 8)).start()
            rest = rest // 8
        weight_sum[...] = jnp.zeros_like(weight_sum)
        total[...] = jnp.zeros_like(total)

        @pl.loop(0, len(MERGED))
        def _(m):
            weight_sum[...] += scatter_sum(
                lambda j: merged[m, j : j + 1, :], lambda j: values[m, j : j + 1, :]
            )

        share = 1.0 / halves(weight_sum[...])
        order = (2, 0, 1, 4, 3)
        steps = list(enumerate(zip(order, order[::-1])))

        for group in (steps[:2], steps[2:]):
            ready = []
            for k, (m, n) in group:
                ends = [
                    either(x, y) for x, y in zip(MERGED[m], MERGED[n]) if x is not None
                ]
                for d in ends:
                    to_air(d).wait_recv()
                ready.append((k, either(m, n), ends))
            for k, _, ends in ready:
                for q in range(4):
                    d, p = ends[0], 3 - q
                    v = slab(weights, d, q) * rows_in[d, 8 * q : 8 * q + 8, :]
                    if len(ends) == 2:
                        e = ends[1]
                        v = v + reverse_tile(slab(weights, e, p) * rows_in[e, 8 * p : 8 * p + 8, :])
                    values[k, 8 * q : 8 * q + 8, :] = v
            sums = [
                scatter_sum(lambda j: merged[which, j : j + 1, :], lambda j: values[k, j : j + 1, :])
                for k, which, _ in ready
            ]
            total[...] += sum(sums[1:], sums[0])
        out[...] = halves(total[...]) * share
        for e in range(SPAN + 2):
            edge_to_ocean(e).wait_send()
        for d in range(SPAN):
            to_ocean(d).wait_send()

    @pl.when(model == 1)
    def _():
        mine = pl.ds(OWN, ROWS)
        loads = [
            load(marine_slot, codes, 0),
            load(state.at[0], own, 1),
            load(coeff.at[0], win_diag.at[mine], 2),
            load(vertical, win_code.at[mine], 3),
        ]
        greet(
            [(1, at(1)), (1, at(2))]
            + [(0, at(offset)) for offset in (1, 2, 3, 4, 5, -1, -2, -3, -4, 0)]
            + [(1, at(-1)), (1, at(-2))]
        )
        for item in loads:
            item.start()

        def to_windows(source, target, send, recv):
            return [
                copy_to(source(first, rows), target(place, rows), send.at[k], recv.at[k], 1, at(offset))
                for k, (offset, first, rows, place) in enumerate(
                    (
                        (1, 0, 16, OWN - 16),
                        (-1, 0, 16, OWN + 16),
                        (2, 8, 8, OWN - 24),
                        (-2, 0, 8, OWN + 32),
                    )
                )
            ]

        ahead = to_windows(
            lambda first, rows: coeff.at[0, pl.ds(first, rows)],
            lambda place, rows: win_diag.at[pl.ds(place, rows)],
            win_send.at[0],
            win_recv.at[0],
        ) + to_windows(
            lambda first, rows: vertical.at[pl.ds(first, rows)],
            lambda place, rows: win_code.at[pl.ds(place, rows)],
            win_send.at[1],
            win_recv.at[1],
        )
        total[...] = jnp.zeros_like(total)
        met(SPAN + 6)
        for item in ahead:
            item.start()
        for item in loads:
            item.wait()

        def edges_here(slots):
            for e in slots:
                edge_to_ocean(e).wait_recv()

        @pl.when(is_last == 0)
        def _():
            edges_here(range(4, 10))

        @pl.when(is_first == 0)
        def _():
            edges_here(range(0, 4))

        @pl.when(is_last == 1)
        def _():
            edges_here(range(4, 5))

        def take(i, rest):
            @pl.when((is_first == 1) & (i == 2))
            def _():
                edges_here(range(0, 4))

            @pl.when((is_last == 1) & (i == 1))
            def _():
                edges_here(range(5, 10))

            pair = (lax.rem(rest, 8), lax.rem(rest // 8, 8))
            for d in pair:
                to_ocean(d).wait_recv()
            for k, d in enumerate(pair):
                above, here, below = edges.at[7 - d], edges.at[8 - d], edges.at[9 - d]
                sides = [
                    here[4:5, :] + above[2:3, :],
                    here[5:6, :] + above[3:4, :],
                    here[6:7, :] + below[0:1, :],
                    here[7:8, :] + below[1:2, :],
                ]
                for q in range(4):
                    column = rows_in[d, 32 + 8 * q : 40 + 8 * q, :].astype(jnp.int32)
                    factor = jnp.where(column < INNER, edge_lookup(sides, column), 1.0)
                    values[k, 8 * q : 8 * q + 8, :] = rows_in[d, 8 * q : 8 * q + 8, :] * factor
            sums = [
                scatter_sum(
                    lambda j: codes[pl.ds(8 * j + d, 1), :], lambda j: values[k, j : j + 1, :], by_parity
                )
                for k, d in enumerate(pair)
            ]
            total[...] += sums[0] + sums[1]
            return rest // 64

        lax.fori_loop(0, SPAN // 2, take, row_order)
        both = total[0:32] + total[32:64]
        for k in (0, 1):
            for h, x in enumerate(even_odd(own, 8 * k)):
                part = slice(16 * h + 8 * k, 16 * h + 8 * k + 8)
                win_rhs[h, OWN + 8 * k : OWN + 8 * k + 8, :] = both[part] + x
                table[8 * k : 8 * k + 8, h * LANES : (h + 1) * LANES] = x - 0.25 * both[part]
        sides = to_windows(
            lambda first, rows: win_rhs.at[:, pl.ds(OWN + first, rows)],
            lambda place, rows: win_rhs.at[:, pl.ds(place, rows)],
            rhs_send,
            rhs_recv,
        )
        for item in sides:
            item.start()
        for item in ahead:
            item.wait_recv()
        for k in range(WINDOW // 8):
            for h, x in enumerate(even_odd(win_diag, 8 * k)):
                scale[h, 8 * k : 8 * k + 8, :] = 1.0 / (x + 3.0)
            for h, x in enumerate(even_odd(win_code, 8 * k)):
                turns[h, 8 * k : 8 * k + 8, :] = x
        def tiles(depth):
            return [pl.ds(OWN + ROWS // 2 - 4 * depth + i, 8, stride=depth) for i in range(depth)]

        for n, (depth, _) in enumerate(STAGES):
            for h in (0, 1):
                for i, rows in enumerate(tiles(depth)):
                    code = turns[h, rows, :]
                    ahead_row = jnp.where(code >= 3, 1, 0)
                    tile_far[n, h, i] = ahead_row
                    tile_side[n, h, i] = code - 3 * ahead_row
                    tile_scale[n, h, i] = scale[h, rows, :]
        for item in sides:
            item.wait_recv()
        for n, (depth, _) in enumerate(STAGES):
            for h in (0, 1):
                for i, rows in enumerate(tiles(depth)):
                    tile_first[n, h, i] = win_rhs[h, rows, :] * tile_scale[n, h, i]

        def sweep(n, eta):
            depth = STAGES[n][0]
            even, odd = list(eta[:depth]), list(eta[depth:])
            before = [pltpu.roll(x, 1, 1) for x in odd]
            after = [pltpu.roll(x, LANES - 1, 1) for x in even]

            def extended(x):
                return [pltpu.roll(x[-1], 1, 0)] + x + [pltpu.roll(x[0], 7, 0)]

            even, odd, before, after = map(extended, (even, odd, before, after))
            result = []
            for h, (left, middle, right) in enumerate(((before, even, odd), (even, odd, after))):
                for i in range(depth):
                    far = tile_far[n, h, i] == 1
                    side = tile_side[n, h, i]
                    x, y, z = (jnp.where(far, v[i + 2], v[i]) for v in (left, middle, right))
                    third = jnp.where(side == 0, x, jnp.where(side == 1, y, z))
                    near = left[i + 1] + right[i + 1] + third
                    result.append(tile_first[n, h, i] + near * tile_scale[n, h, i])
            return tuple(result)

        for n, (depth, count) in enumerate(STAGES):
            if n == 0:
                eta = tuple(tile_first[0, h, i] for h in (0, 1) for i in range(depth))
            else:
                eta = tuple(scale[h, rows, :] for h in (0, 1) for rows in tiles(depth))
            eta = lax.fori_loop(0, count, lambda _, x: sweep(n, x), eta)
            for h in (0, 1):
                for i, rows in enumerate(tiles(depth)):
                    scale[h, rows, :] = eta[depth * h + i]
        mine_eta = [scale[h, OWN : OWN + ROWS, :] for h in (0, 1)]
        table[...] = table[...] + 0.5 * jnp.concatenate(mine_eta, axis=1)
        start = is_last * (3 - lax.rem(tile, 4))
        back = (3, 2, 1, 0, 6, 7, 5, 4)
        rest = in_order((5, 6, 7, 2, 0, 1, 3, 4), (3, 2, 0, 1, 6, 7, 5, 4), back)
        def give(i, rest):
            for k in range(2):
                d = lax.rem(rest, 8)
                rest = rest // 8
                back_turn = is_last * ((SPAN - 1 - (2 * i + k)) // 4)
                d = d + back_turn * (lax.rem(d - start + 4, 4) - d)
                for q in range(4):
                    rows_out[d, 8 * q : 8 * q + 8, :] = lookup(table, slab(codes, d, q), by_parity)
                to_air(d).start()
            return rest

        lax.fori_loop(0, SPAN // 2, give, rest)
        for k in (0, 1):
            rows = slice(8 * k, 8 * k + 8)
            out[rows, :] = interleaved(mine_eta[0][rows], mine_eta[1][rows])
        for item in ahead + sides:
            item.wait_send()
        for d in range(SPAN):
            to_air(d).wait_send()


def shards(state, coeff, vertical, send_cell, incoming_marine_slot, remap_weight):
    def blocks(x):
        return x.reshape(SPAN, BLOCKS, LANES).transpose(1, 0, 2).reshape(SPAN * BLOCKS, LANES)

    anywhere = pl.BlockSpec(memory_space=pltpu.HBM)
    grid = pltpu.VMEM((ROWS, COLS), F32)
    dma = pltpu.SemaphoreType.DMA
    result = pl.pallas_call(
        kernel,
        out_shape=jax.ShapeDtypeStruct((ROWS, COLS), F32),
        in_specs=[anywhere] * 6,
        out_specs=pl.BlockSpec(memory_space=pltpu.VMEM),
        scratch_shapes=[
            grid,
            grid,
            grid,
            pltpu.VMEM((SPAN * BLOCKS, LANES), jnp.int32),
            pltpu.VMEM((SPAN * BLOCKS, LANES), F32),
            pltpu.VMEM((8, LANES), F32),
            pltpu.VMEM((SPAN + 2, 8, LANES), F32),
            pltpu.VMEM((len(MERGED), BLOCKS, LANES), jnp.int32),
            pltpu.VMEM((len(MERGED), BLOCKS, LANES), F32),
            pltpu.VMEM((SPAN, 2 * BLOCKS, LANES), F32),
            pltpu.VMEM((SPAN, 2 * BLOCKS, LANES), F32),
            pltpu.VMEM((64, LANES), F32),
            pltpu.VMEM((64, LANES), F32),
            pltpu.VMEM((2, WINDOW, LANES), F32),
            pltpu.VMEM((WINDOW, COLS), F32),
            pltpu.VMEM((WINDOW, COLS), jnp.int32),
            pltpu.VMEM((2, WINDOW, LANES), F32),
            pltpu.VMEM((2, WINDOW, LANES), jnp.int32),
            pltpu.VMEM((len(STAGES), 2, STAGES[0][0], 8, LANES), F32),
            pltpu.VMEM((len(STAGES), 2, STAGES[0][0], 8, LANES), F32),
            pltpu.VMEM((len(STAGES), 2, STAGES[0][0], 8, LANES), jnp.int32),
            pltpu.VMEM((len(STAGES), 2, STAGES[0][0], 8, LANES), jnp.int32),
            dma((4,)),
            dma((SPAN + 2,)),
            dma((SPAN + 2,)),
            dma((SPAN,)),
            dma((SPAN,)),
            dma((4,)),
            dma((4,)),
            dma((2, 4)),
            dma((2, 4)),
        ],
        compiler_params=pltpu.CompilerParams(
            collective_id=0, has_side_effects=True, vmem_limit_bytes=40 << 20
        ),
    )(
        *(
            pltpu.with_memory_space_constraint(x, pltpu.HBM)
            for x in (
                state,
                coeff,
                vertical,
                blocks(send_cell),
                blocks(incoming_marine_slot),
                blocks(remap_weight),
            )
        )
    )
    return result[None]


def solution(mesh):
    in_specs = (
        P("comp", "tile", None),
        P("comp", "tile", None),
        P("tile", None),
        P(("comp", "tile"), None),
        P(("comp", "tile"), None),
        P(("comp", "tile"), None),
    )
    out_specs = P("comp", "tile", None)
    return jax.shard_map(shards, mesh=mesh, in_specs=in_specs, out_specs=out_specs, check_vma=False)
```
